128 devices in a mesh: gx: 8 (over x, core), gy: 16 (over y, z).
Axes of the slice: x: 4, y: 4, z: 4, core: 2. Of those that a mesh axis runs over, the one named last changes fastest.
Arguments:
- feats: bfloat16 [524288, 192], P(('gx', 'gy')), may hold values from -6 to 6
- conv_weight: bfloat16 [27, 192, 192], replicated, may hold values from -0.125 to 0.125
- tap_index: int32 [524288, 27], P(('gx', 'gy')), may hold values from -1 to 8191, as said below
- halo_rows: int32 [128, 8, 512], P(('gx', 'gy')), may hold values from -1 to 4095, as said below
- hilbert_pos: int32 [524288], P(('gx', 'gy')), may hold values from 0 to 524287, as said below
- ln1_gain: float32 [192], replicated, may hold values from 0.1 to 1.9
- qkv_weight: bfloat16 [192, 576], replicated
- out_weight: bfloat16 [192, 192], replicated, may hold values from -0.4375 to 0.4375
- ln2_gain: float32 [192], replicated, may hold values from 0.1 to 1.9
- mlp_in: bfloat16 [192, 768], replicated, may hold values from -0.4375 to 0.4375
- mlp_out: bfloat16 [768, 192], replicated, may hold values from -0.21875 to 0.21875
Outputs:
- result: bfloat16 [524288, 192], P(('gx', 'gy'))
The draws below stay inside these ranges and needn't reach their ends.
Inputs may be any that keep to these rules, and one draw needn't show every extreme that they name: `tap_index`: tap 13 of each point is the point's own row; below 4096: a row of the device's own points; 4096 + k * 512 + j: slot j of incoming list k. Within each aligned block of 128 points of a device and for each offset, all entries other than -1 lie in one aligned group of 128 rows of the lookup table (rows 128 g to 128 g + 127). `halo_rows`: -1 marks an empty slot; live slots of a list come first; every device has one list with all 512 slots live. `hilbert_pos`: A permutation of all points; device d's Hilbert range is positions d * 4096 to (d + 1) * 4096 - 1, with devices numbered x * 16 + y. Each point falls in the range of its own device or of a device whose x and y differ from its own by at most 1; at most 256 points of one device fall in one other device's range, exactly 256 for some pair in every draw.
All inputs are finite; a program needn't handle non-finite values.
Results may differ from the reference program's by a relative error of at most 0.0096.
Values may be sent and summed in bfloat16 or wider, within the bound.
A program may use at most 128 MiB of HBM per device.

```python
import math
import jax
import jax.numpy as jnp
from jax import lax

C = 192
HEADS = 8
HID = 768
WIN = 1024
TAPS = 27
P_DEV = 4096
HB = 512
NPTS = 524288
N_GX = 8
N_GY = 16


def draw_tap_index(key, part):
    first_key, second_key, third_key = jax.random.split(key, 3)
    tile_total = NPTS // 128
    group_total = (P_DEV + 8 * HB) // 128
    live_draw = jax.random.randint(first_key, (NPTS, TAPS), 0, 5) < 2
    tile_group = jax.random.randint(third_key, (tile_total, TAPS), 0, group_total)
    own_tile = (jnp.arange(tile_total, dtype=jnp.int32) % (P_DEV // 128)).astype(jnp.int32)
    tile_group = tile_group.at[:, 13].set(own_tile)
    row_group = jnp.repeat(tile_group, 128, axis=0)
    targets = row_group * 128 + jax.random.randint(second_key, (NPTS, TAPS), 0, 128)
    chosen = jnp.where(live_draw, targets, -1)
    own_rows = (jnp.arange(NPTS, dtype=jnp.int32) % P_DEV).astype(jnp.int32)
    return chosen.at[:, 13].set(own_rows).astype(jnp.int32)


def draw_halo_rows(key, part):
    first_key, second_key, third_key = jax.random.split(key, 3)
    devices = N_GX * N_GY
    live_count = jax.random.randint(first_key, (devices, 8), HB // 4, HB + 1)
    full_list = jax.random.randint(second_key, (devices,), 0, 8)
    live_count = jnp.where(jnp.arange(8)[None, :] == full_list[:, None], HB, live_count)
    chosen = jax.random.randint(third_key, (devices, 8, HB), 0, P_DEV)
    return jnp.where(jnp.arange(HB)[None, None, :] < live_count[:, :, None], chosen, -1).astype(jnp.int32)


def draw_hilbert_pos(key, part):
    first_key, second_key, third_key = jax.random.split(key, 3)
    devices = N_GX * N_GY
    most = P_DEV // 16
    index = jnp.arange(devices, dtype=jnp.int32)
    row_x = index // N_GY
    row_y = index % N_GY
    near = (jnp.abs(row_x[:, None] - row_x[None, :]) <= 1) & (jnp.abs(row_y[:, None] - row_y[None, :]) <= 1) & (index[:, None] != index[None, :])
    raw = jax.random.randint(first_key, (devices, devices), most // 4, most + 1)
    symmetric = jnp.where(index[:, None] < index[None, :], raw, raw.T)
    symmetric = symmetric.at[0, 1].set(most).at[1, 0].set(most)
    moving = jnp.where(near, symmetric, 0).astype(jnp.int32)
    kept = P_DEV - jnp.sum(moving, 1)
    pair_counts = moving + jnp.where(index[:, None] == index[None, :], kept[:, None], 0).astype(jnp.int32)
    ends = jnp.cumsum(pair_counts, 1)
    slots = jnp.arange(P_DEV, dtype=jnp.int32)
    sorted_target = jax.vmap(lambda edge: jnp.searchsorted(edge, slots, side='right'))(ends).astype(jnp.int32)
    shuffle_keys = jax.random.split(second_key, devices)
    target = jax.vmap(lambda shuffle_key, row_target: jax.random.permutation(shuffle_key, row_target))(shuffle_keys, sorted_target).reshape(-1)
    mixing = jax.random.permutation(third_key, NPTS)
    order = jnp.argsort(target[mixing], stable=True)
    sorted_points = mixing[order]
    return jnp.zeros((NPTS,), jnp.int32).at[sorted_points].set(jnp.arange(NPTS, dtype=jnp.int32))


def draw_qkv_weight(key, part):
    first_key, second_key, third_key = jax.random.split(key, 3)
    scaling = C ** (-0.5)
    queries = jax.random.normal(first_key, (C, C), jnp.float32) * scaling
    values = jax.random.normal(third_key, (C, C), jnp.float32) * scaling
    key_block = jax.random.normal(second_key, (C, C), jnp.float32) * scaling
    return jnp.concatenate([queries, key_block, values], 1).astype(jnp.bfloat16)


def level_of(own_key, extent, shards, least, top_value):
    factor_of = 1.0
    for dim, shards_of in shards:
        steps = jax.random.uniform(jax.random.fold_in(jax.random.fold_in(own_key, 6), dim), (shards_of,), jnp.float32, least / len(shards), top_value / len(shards))
        factor_of = factor_of * jnp.repeat(jnp.exp(steps), extent[dim] // shards_of).reshape((-1,) + (1,) * (len(extent) - 1 - dim))
    return factor_of


def noise(own_key, extent, spread, most, shards=(), kind=jnp.bfloat16):
    drawn = spread * jax.random.normal(own_key, extent, jnp.float32)
    if shards:
        drawn = drawn * level_of(own_key, extent, shards, -0.22, 0.18)
    return jnp.clip(drawn, -most, most).astype(kind)


def setup_inputs(seed: int = 0) -> dict:
    arg_keys = jax.random.split(jax.random.key(seed), 12)
    return {
        "feats": noise(arg_keys[0], (NPTS, C), 1.0, 6.0, ((0, 128),)),
        "conv_weight": noise(arg_keys[1], (TAPS, C, C), (10 * C) ** -0.5, 0.125),
        "tap_index": draw_tap_index(jax.random.fold_in(arg_keys[11], 71), 0),
        "halo_rows": draw_halo_rows(jax.random.fold_in(arg_keys[11], 71), 0),
        "hilbert_pos": draw_hilbert_pos(jax.random.fold_in(arg_keys[11], 71), 0),
        "ln1_gain": jnp.clip(1.0 + 0.18 * jax.random.normal(arg_keys[5], (C,), jnp.float32), 0.1, 1.9),
        "qkv_weight": draw_qkv_weight(jax.random.fold_in(arg_keys[11], 71), 0),
        "out_weight": noise(arg_keys[7], (C, C), C ** -0.5, 0.4375),
        "ln2_gain": jnp.clip(1.0 + 0.18 * jax.random.normal(arg_keys[8], (C,), jnp.float32), 0.1, 1.9),
        "mlp_in": noise(arg_keys[9], (C, HID), C ** -0.5, 0.4375),
        "mlp_out": noise(arg_keys[10], (HID, C), HID ** -0.5, 0.21875),
    }


OFFSETS = ((-1, -1), (-1, 0), (-1, 1), (0, -1), (0, 1), (1, -1), (1, 0), (1, 1))

def layer_norm(values, gain):
    widened = values.astype(jnp.float32)
    average = lax.optimization_barrier(jnp.mean(widened, -1, keepdims=True))
    centred = widened - average
    variance = lax.optimization_barrier(jnp.mean(centred * centred, -1, keepdims=True))
    return (centred * lax.rsqrt(variance + 1e-05) * gain).astype(jnp.bfloat16)

def window_block(window, ln1_gain, qkv_weight, out_weight, ln2_gain, mlp_in, mlp_out):
    row_count, channels = window.shape
    head_dim = channels // HEADS
    normed = layer_norm(window, ln1_gain)
    packed = jnp.dot(normed, qkv_weight, preferred_element_type=jnp.float32).astype(jnp.bfloat16)
    queries = packed[:, :channels].reshape(row_count, HEADS, head_dim).transpose(1, 0, 2)
    key_rows = packed[:, channels:2 * channels].reshape(row_count, HEADS, head_dim).transpose(1, 0, 2)
    values = packed[:, 2 * channels:].reshape(row_count, HEADS, head_dim).transpose(1, 0, 2)
    scaling = 1.0 / math.sqrt(head_dim)

    def one_head(triple):
        query_head, key_head, value_head = triple
        scores = jnp.dot(query_head, key_head.T, preferred_element_type=jnp.float32) * scaling
        weights = jax.nn.softmax(scores, axis=-1).astype(jnp.bfloat16)
        return jnp.dot(weights, value_head, preferred_element_type=jnp.float32).astype(jnp.bfloat16)
    attended = lax.map(one_head, (queries, key_rows, values)).transpose(1, 0, 2).reshape(row_count, channels)
    residual = (window.astype(jnp.float32) + jnp.dot(attended, out_weight, preferred_element_type=jnp.float32)).astype(jnp.bfloat16)
    normed_two = layer_norm(residual, ln2_gain)
    hidden = jax.nn.gelu(jnp.dot(normed_two, mlp_in, preferred_element_type=jnp.float32), approximate=False).astype(jnp.bfloat16)
    return (residual.astype(jnp.float32) + jnp.dot(hidden, mlp_out, preferred_element_type=jnp.float32)).astype(jnp.bfloat16)

def reference(feats, conv_weight, tap_index, halo_rows, hilbert_pos, ln1_gain, qkv_weight, out_weight, ln2_gain, mlp_in, mlp_out):
    devices = N_GX * N_GY
    blocks = feats.reshape(N_GX, N_GY, P_DEV, C)
    lists = halo_rows.reshape(N_GX, N_GY, 8, HB)
    picked = jax.vmap(jax.vmap(lambda block, chosen: block[jnp.maximum(chosen, 0)]))(blocks, lists)
    outgoing = jnp.where((lists >= 0)[..., None], picked, jnp.zeros_like(picked))
    padded = jnp.pad(outgoing, ((1, 1), (1, 1), (0, 0), (0, 0), (0, 0)))
    incoming = jnp.stack([padded[1 + step_x:1 + step_x + N_GX, 1 + step_y:1 + step_y + N_GY, 7 - number] for number, (step_x, step_y) in enumerate(OFFSETS)], 2)
    lookup = jnp.concatenate([blocks, incoming.reshape(N_GX, N_GY, 8 * HB, C), jnp.zeros((N_GX, N_GY, 1, C), feats.dtype)], 2).reshape(devices, P_DEV + 8 * HB + 1, C)
    taps = tap_index.reshape(devices, P_DEV, TAPS)
    taps = jnp.where(taps < 0, P_DEV + 8 * HB, taps).astype(jnp.int32)
    flat_weight = conv_weight.reshape(TAPS * C, C)

    def conv_device(pair):
        device_table, device_taps = pair
        gathered = device_table[device_taps].reshape(P_DEV, TAPS * C)
        return jnp.dot(gathered, flat_weight, preferred_element_type=jnp.float32)
    conv_out = lax.map(conv_device, (lookup, taps)).reshape(NPTS, C)
    updated = (feats.astype(jnp.float32) + conv_out).astype(jnp.bfloat16)
    ordered = jnp.zeros((NPTS, C), updated.dtype).at[hilbert_pos].set(updated)
    windows = ordered.reshape(NPTS // WIN, WIN, C)
    processed = lax.map(lambda window: window_block(window, ln1_gain, qkv_weight, out_weight, ln2_gain, mlp_in, mlp_out), windows)
    return processed.reshape(NPTS, C)[hilbert_pos]
```

```python
import functools
import math

import jax
import jax.numpy as jnp
from jax import lax
from jax.experimental import pallas as pl
from jax.experimental.pallas import tpu as pltpu
from jax.sharding import PartitionSpec as P

BF = jnp.bfloat16
F32 = jnp.float32
I32 = jnp.int32
MESH = pl.DeviceIdType.MESH

C = 192
HEADS = 8
HD = 24
HP = 32
WIN = 1024
TAPS = 27
PTS = 4096
HB = 512
CAP = PTS // 16
SLAB = CAP + CAP // 2
OFFSETS = ((-1, -1), (-1, 0), (-1, 1), (0, -1), (0, 1), (1, -1), (1, 0), (1, 1))
SEND_ORDER = (0, 7, 2, 5, 3, 4, 1, 6)
DUMP = PTS
TALL = PTS + 8
SPOT_STRIDE = 1024
SPOTS = 8 * SPOT_STRIDE
VMEM_LIMIT = 60 * 1024 * 1024
SCALE = 1.0 / math.sqrt(HD) * math.log2(math.e)
SAFE = 80.0


def params(**kw):
    return pltpu.CompilerParams(vmem_limit_bytes=VMEM_LIMIT, **kw)


VM = pl.BlockSpec(memory_space=pltpu.VMEM)
SM = pl.BlockSpec(memory_space=pltpu.SMEM)
ANY = pl.BlockSpec(memory_space=pl.ANY)


def prep_kernel(
    hp_ref, tap_ref, cw_ref, halo_ref, qkvw_ref, ow_ref, g1_ref, g2_ref, w1_ref,
    fetch_ref, sidx_ref, spot_ref, group_ref, hidx_ref, cwt_ref, qkvt_ref, owt_ref,
    g1c_ref, g2c_ref, w1t_ref, pad,
):
    ix = lax.axis_index("gx")
    iy = lax.axis_index("gy")
    ny = lax.axis_size("gy")
    hp = hp_ref[...]
    target = hp // PTS
    local = hp - target * PTS
    step_x = target // ny - ix
    step_y = target % ny - iy
    code = 3 * (step_x + 1) + (step_y + 1)
    r128 = lax.broadcasted_iota(I32, (128, 128), 0)
    c128 = lax.broadcasted_iota(I32, (128, 128), 1)
    tri = (r128 < c128).astype(F32).astype(BF)
    r32 = lax.broadcasted_iota(I32, (32, 32), 0)
    c32 = lax.broadcasted_iota(I32, (32, 32), 1)
    low = (c32 < r32).astype(F32).astype(BF)
    before = jnp.zeros((32, 128), F32)
    for c in range(9):
        if c == 4:
            continue
        m = (code == c).astype(F32)
        mb = m.astype(BF)
        within = jnp.dot(mb, tri, preferred_element_type=F32)
        above = jnp.sum(jnp.dot(low, mb, preferred_element_type=F32), 1, keepdims=True)
        before = before + m * (within + above)
    rank = before.astype(I32)
    number = code - (code > 4).astype(I32)
    own = code == 4
    fetch_ref[...] = jnp.where(own, local, PTS + number * CAP + rank)
    sidx_ref[...] = jnp.where(own, SPOTS, number * SPOT_STRIDE + rank)
    spot_ref[...] = local
    halo = halo_ref[...]
    hidx_ref[...] = jnp.where(halo < 0, DUMP, halo)

    lane = lax.broadcasted_iota(I32, (TAPS, 128), 1)
    groups = jnp.zeros((TAPS, 128), I32)
    for i in range(PTS // 128):
        top = jnp.max(tap_ref[:, i * 128 : (i + 1) * 128], 1, keepdims=True)
        groups = jnp.where(lane == i, jnp.maximum(top, 0) // 128, groups)
    group_ref[...] = groups

    for i in range(0, TAPS * C, 384):
        size = min(384, TAPS * C - i)
        cwt_ref[:, i : i + size] = cw_ref[i : i + size, :].astype(F32).T.astype(BF)

    wide = qkvw_ref[...].astype(F32).T
    pad[...] = jnp.zeros_like(pad)
    for j in range(3 * HEADS):
        pad[j * HP : j * HP + HD, :] = wide[j * HD : (j + 1) * HD, :]
    qkvt_ref[...] = pad[...].astype(BF)
    ow = ow_ref[...].astype(F32)
    for j in range(HEADS):
        pad[j * HP : j * HP + HD, :] = ow[j * HD : (j + 1) * HD, :]
    owt_ref[...] = pad[0 : HEADS * HP, :].T.astype(BF)
    g1c_ref[...] = jnp.broadcast_to(g1_ref[...], (128, C)).T
    g2c_ref[...] = jnp.broadcast_to(g2_ref[...], (128, C)).T
    w1t_ref[...] = w1_ref[...].astype(F32).T.astype(BF)


def prep(hp, tap_t, cw, halo, qkvw, ow, g1, g2, w1):
    sd = jax.ShapeDtypeStruct
    return pl.pallas_call(
        prep_kernel,
        name="prep",
        in_specs=[VM] * 9,
        out_specs=[VM] * 11,
        out_shape=[
            sd((32, 128), I32), sd((32, 128), I32), sd((32, 128), I32),
            sd((TAPS, 128), I32), sd((32, 128), I32), sd((C, TAPS * C), BF),
            sd((3 * HEADS * HP, C), BF), sd((C, HEADS * HP), BF),
            sd((C, 128), F32), sd((C, 128), F32), sd((4 * C, C), BF),
        ],
        scratch_shapes=[pltpu.VMEM((3 * HEADS * HP, C), F32)],
        compiler_params=params(),
    )(hp, tap_t, cw, halo, qkvw, ow, g1, g2, w1)


def neighbours():
    ix = lax.axis_index("gx")
    iy = lax.axis_index("gy")
    nx = lax.axis_size("gx")
    ny = lax.axis_size("gy")
    found = []
    for a, b in OFFSETS:
        x = ix + a
        y = iy + b
        inside = (x >= 0) & (x < nx) & (y >= 0) & (y < ny)
        found.append((inside, x, y))
    return found


def greet(near):
    barrier = pltpu.get_barrier_semaphore()
    for inside, x, y in near:
        @pl.when(inside)
        def _():
            pl.semaphore_signal(barrier, inc=1, device_id=(x, y), device_id_type=MESH)
    return barrier


def meet(barrier, near):
    count = sum(inside.astype(I32) for inside, _, _ in near)
    pl.semaphore_wait(barrier, count)


def push(k, near, src, dst, send_sem, recv_sem):
    _, x, y = near[k]
    return pltpu.make_async_remote_copy(
        src_ref=src, dst_ref=dst, send_sem=send_sem.at[k], recv_sem=recv_sem.at[7 - k],
        device_id=(x, y), device_id_type=MESH,
    )


def halo_kernel(idx_ref, feats_ref, out_ref, table, rows, send, zeros, send_sem, recv_sem, zero_sem):
    near = neighbours()
    barrier = greet(near)

    def turn(i, carry):
        at = pl.multiple_of(i * 128, 128)
        table[pl.ds(at, 128), :] = feats_ref[:, pl.ds(at, 128)].astype(F32).T
        return carry

    lax.fori_loop(0, PTS // 128, turn, 0)
    table[PTS:TALL, :] = jnp.zeros((TALL - PTS, C), F32)
    zeros[...] = jnp.zeros_like(zeros)
    meet(barrier, near)

    def gather(k, first, last):
        def block(b, carry):
            at = pl.multiple_of(b * 16, 16)
            got = [table[pl.ds(idx_ref[k * HB + at + u], 1), :] for u in range(16)]
            rows[pl.ds(at, 16), :] = jnp.concatenate(got, 0)
            return carry

        lax.fori_loop(first, last, block, 0)

    def start(k):
        @pl.when(near[k][0])
        def _():
            push(k, near, send.at[k], out_ref.at[7 - k], send_sem, recv_sem).start()

        @pl.when(jnp.logical_not(near[k][0]))
        def _():
            pltpu.make_async_copy(zeros, out_ref.at[k], zero_sem.at[k]).start()

    previous = None
    for k in SEND_ORDER:
        gather(k, 0, 8)
        if previous is not None:
            start(previous)
        gather(k, 8, HB // 16)
        for c in range(HB // 128):
            send[k, :, c * 128 : (c + 1) * 128] = rows[c * 128 : (c + 1) * 128, :].T.astype(BF)
        previous = k
    start(previous)

    for k in SEND_ORDER:
        @pl.when(near[k][0])
        def _():
            push(k, near, send.at[k], out_ref.at[7 - k], send_sem, recv_sem).wait_send()
            push(7 - k, near, send.at[k], out_ref.at[k], send_sem, recv_sem).wait_recv()

        @pl.when(jnp.logical_not(near[k][0]))
        def _():
            pltpu.make_async_copy(zeros, out_ref.at[k], zero_sem.at[k]).wait()


def halo_exchange(idx, feats_t):
    return pl.pallas_call(
        halo_kernel,
        name="halo_exchange",
        in_specs=[SM, VM],
        out_specs=ANY,
        out_shape=jax.ShapeDtypeStruct((8, C, HB), BF),
        scratch_shapes=[
            pltpu.VMEM((TALL, C), F32),
            pltpu.VMEM((HB, C), F32),
            pltpu.VMEM((8, C, HB), BF),
            pltpu.VMEM((C, HB), BF),
            pltpu.SemaphoreType.DMA((8,)),
            pltpu.SemaphoreType.DMA((8,)),
            pltpu.SemaphoreType.DMA((8,)),
        ],
        compiler_params=params(collective_id=0, has_side_effects=True),
    )(idx, feats_t)


STEP = 4
CONV_STEPS = PTS // (128 * STEP)


def conv_kernel(
    group_ref, fetch_ref, sidx_ref, spot_ref, tap_ref, cwt_ref, feats_ref, halo_ref,
    own_ref, slab_ref, spots_ref, lookup, gathered, table, rows, slabs, load_sem, out_sem,
):
    i = pl.program_id(0)

    @pl.when(i == 0)
    def _():
        copies = [pltpu.make_async_copy(feats_ref, lookup.at[:, 0:PTS], load_sem.at[8])]
        for k in range(8):
            at = PTS + k * HB
            copies.append(
                pltpu.make_async_copy(halo_ref.at[k], lookup.at[:, at : at + HB], load_sem.at[k])
            )
        for copy in copies:
            copy.start()

        def clear(b, carry):
            for k in range(8):
                for u in range(8):
                    spots_ref[k * SPOT_STRIDE + b * 8 + u] = DUMP
            return carry

        lax.fori_loop(0, CAP // 8, clear, 0)
        for copy in copies:
            copy.wait()

    for n in range(STEP):
        def tap(t, carry):
            start = pl.multiple_of(group_ref[t, i * STEP + n] * 128, 128)
            source = lookup[:, pl.ds(start, 128)].astype(F32)
            index = jnp.broadcast_to(tap_ref[pl.ds(t, 1), n * 128 : (n + 1) * 128], (C, 128))
            taken = jnp.take_along_axis(source, index & 127, axis=1)
            taken = jnp.where(index >= 0, taken, 0.0)
            gathered[pl.ds(pl.multiple_of(t * C, C), C), n * 128 : (n + 1) * 128] = taken.astype(BF)
            return carry

        lax.fori_loop(0, TAPS, tap, 0, unroll=True)
    conv = jnp.dot(cwt_ref[...], gathered[...], preferred_element_type=F32)
    here = lookup[:, pl.ds(pl.multiple_of(i * (128 * STEP), 128), 128 * STEP)].astype(F32)
    rows[...] = (here + conv).astype(BF).astype(F32).T

    def scatter(b, carry):
        at = b * 16
        for u in range(16):
            p = i * (128 * STEP) + at + u
            table[pl.ds(fetch_ref[p], 1), :] = rows[pl.ds(at + u, 1), :]
            spots_ref[sidx_ref[p]] = spot_ref[p]
        return carry

    lax.fori_loop(0, 8 * STEP, scatter, 0)

    @pl.when(i == CONV_STEPS - 1)
    def _():
        home = pltpu.make_async_copy(table.at[0:PTS, :], own_ref, out_sem.at[0])
        home.start()
        for k in range(8):
            at = PTS + k * CAP
            slabs[k, 0:CAP, :] = table[at : at + CAP, 0:128].astype(BF)
            half = CAP // 2
            slabs[k, CAP:SLAB, :] = jnp.concatenate(
                [table[at : at + half, 128:C], table[at + half : at + CAP, 128:C]], 1
            ).astype(BF)
        away = pltpu.make_async_copy(slabs, slab_ref, out_sem.at[1])
        away.start()
        home.wait()
        away.wait()


def conv(groups, fetch, sidx, spot, tap_t, cwt, feats_t, halo):
    sd = jax.ShapeDtypeStruct
    return pl.pallas_call(
        conv_kernel,
        name="conv",
        grid=(CONV_STEPS,),
        in_specs=[
            SM, SM, SM, SM,
            pl.BlockSpec((TAPS, 128 * STEP), lambda i: (0, i)),
            pl.BlockSpec((C, TAPS * C), lambda i: (0, 0), pipeline_mode=pl.Buffered(1)),
            ANY, ANY,
        ],
        out_specs=[ANY, ANY, SM],
        out_shape=[sd((PTS, C), F32), sd((8, SLAB, 128), BF), sd((SPOTS + 1024,), I32)],
        scratch_shapes=[
            pltpu.VMEM((C, PTS + 8 * HB), BF),
            pltpu.VMEM((TAPS * C, 128 * STEP), BF),
            pltpu.VMEM((PTS + 8 * CAP, C), F32),
            pltpu.VMEM((128 * STEP, C), F32),
            pltpu.VMEM((8, SLAB, 128), BF),
            pltpu.SemaphoreType.DMA((9,)),
            pltpu.SemaphoreType.DMA((2,)),
        ],
        compiler_params=params(dimension_semantics=("arbitrary",)),
    )(groups, fetch, sidx, spot, tap_t, cwt, feats_t, halo)


def deal_kernel(slab_ref, spots_ref, slab_out, spots_out, send_sem, recv_sem, send_spot, recv_spot):
    near = neighbours()
    barrier = greet(near)
    meet(barrier, near)

    def spot_push(k):
        src = spots_ref.at[pl.ds(k * SPOT_STRIDE, SPOT_STRIDE)]
        dst = spots_out.at[pl.ds((7 - k) * SPOT_STRIDE, SPOT_STRIDE)]
        return push(k, near, src, dst, send_spot, recv_spot)

    for k in SEND_ORDER:
        @pl.when(near[k][0])
        def _():
            push(k, near, slab_ref.at[k], slab_out.at[7 - k], send_sem, recv_sem).start()
            spot_push(k).start()

    for k in SEND_ORDER:
        @pl.when(near[k][0])
        def _():
            push(k, near, slab_ref.at[k], slab_out.at[7 - k], send_sem, recv_sem).wait_send()
            spot_push(k).wait_send()
            push(7 - k, near, slab_ref.at[k], slab_out.at[k], send_sem, recv_sem).wait_recv()
            spot_push(7 - k).wait_recv()


def deal(slabs, spots):
    sd = jax.ShapeDtypeStruct
    return pl.pallas_call(
        deal_kernel,
        name="deal",
        in_specs=[ANY, ANY],
        out_specs=[ANY, ANY],
        out_shape=[sd((8, SLAB, 128), BF), sd((SPOTS,), I32)],
        scratch_shapes=[pltpu.SemaphoreType.DMA((8,))] * 4,
        compiler_params=params(collective_id=1, has_side_effects=True),
    )(slabs, spots)


def norm_columns(values, gain):
    average = jnp.sum(values, 0, keepdims=True) * (1.0 / C)
    centred = values - average
    variance = jnp.sum(centred * centred, 0, keepdims=True) * (1.0 / C)
    return (centred * lax.rsqrt(variance + 1e-05) * gain).astype(BF)


def unpack(slab, rows, at):
    half = CAP // 2
    rows[at : at + CAP, 0:128] = slab[0:CAP, :].astype(F32)
    tail = slab[CAP:SLAB, :].astype(F32)
    rows[at : at + half, 128:C] = tail[:, 0:64]
    rows[at + half : at + CAP, 128:C] = tail[:, 64:128]


def window_kernel(
    spots_ref, own_ref, slab_ref, g1_ref, qkvt_ref, owt_ref, g2_ref, w1t_ref, w2t_ref,
    out_ref, rows, packed, attended, load_sem,
):
    home = pltpu.make_async_copy(own_ref, out_ref.at[0:PTS, :], load_sem)
    home.start()
    near = neighbours()
    for k in range(8):
        @pl.when(near[k][0])
        def _():
            unpack(slab_ref[k], rows, k * CAP)
    home.wait()
    for k in range(8):
        @pl.when(near[k][0])
        def _():
            def place(b, carry):
                at = b * 16
                for u in range(16):
                    spot = spots_ref[k * SPOT_STRIDE + at + u]
                    out_ref[pl.ds(spot, 1), :] = rows[pl.ds(k * CAP + at + u, 1), :]
                return carry

            lax.fori_loop(0, CAP // 16, place, 0)

    def window(w, carry):
        base = pl.multiple_of(w * WIN, WIN)
        x = out_ref[pl.ds(base, WIN), :].T
        normed = norm_columns(x, g1_ref[:, 0:1])
        wide = HEADS * HP
        queries = jnp.dot(qkvt_ref[0:wide, :], normed, preferred_element_type=F32) * SCALE
        packed[0:wide, :] = queries.astype(BF)
        packed[wide : 3 * wide, :] = jnp.dot(
            qkvt_ref[wide : 3 * wide, :], normed, preferred_element_type=F32
        ).astype(BF)
        largest_q = jnp.zeros((1, WIN), F32)
        largest_k = jnp.zeros((1, WIN), F32)
        for h in range(HEADS):
            q = packed[h * HP : (h + 1) * HP, :].astype(F32)
            key = packed[wide + h * HP : wide + (h + 1) * HP, :].astype(F32)
            largest_q = jnp.maximum(largest_q, jnp.sum(q * q, 0, keepdims=True))
            largest_k = jnp.maximum(largest_k, jnp.sum(key * key, 0, keepdims=True))
        safe = jnp.max(largest_q) * jnp.max(largest_k) <= SAFE * SAFE

        def heads(shifted):
            def head(h, inner):
                off = pl.multiple_of(h * HP, HP)
                q = packed[pl.ds(off, HP), :]
                key = packed[pl.ds(wide + off, HP), :]
                value = packed[pl.ds(2 * wide + off, HP), :]
                number = lax.broadcasted_iota(I32, (HP, WIN), 0)
                value = jnp.where(number == HD, jnp.ones_like(value), value)
                scores = lax.dot_general(
                    key, q, (((0,), (0,)), ((), ())), preferred_element_type=F32
                )
                if shifted:
                    scores = scores - jnp.max(scores, 0, keepdims=True)
                probs = jnp.exp2(scores).astype(BF)
                mixed = jnp.dot(value, probs, preferred_element_type=F32)
                attended[pl.ds(off, HP), :] = (mixed / mixed[HD : HD + 1, :]).astype(BF)
                return inner

            lax.fori_loop(0, HEADS, head, 0, unroll=1 if shifted else 2)

        @pl.when(safe)
        def _():
            heads(False)

        @pl.when(jnp.logical_not(safe))
        def _():
            heads(True)

        residual = x + jnp.dot(owt_ref[...], attended[...], preferred_element_type=F32)
        residual = residual.astype(BF).astype(F32)
        normed_two = norm_columns(residual, g2_ref[:, 0:1])
        hidden = jnp.dot(w1t_ref[...], normed_two, preferred_element_type=F32)
        hidden = 0.5 * hidden * (1.0 + lax.erf(hidden * (2.0**-0.5)))
        processed = residual + jnp.dot(w2t_ref[...], hidden.astype(BF), preferred_element_type=F32)
        out_ref[pl.ds(base, WIN), :] = processed.astype(BF).astype(F32).T
        return carry

    lax.fori_loop(0, PTS // WIN, window, 0)


def windows(spots, own, slabs, g1, qkvt, owt, g2, w1t, w2t):
    return pl.pallas_call(
        window_kernel,
        name="windows",
        in_specs=[SM, ANY, VM, VM, VM, VM, VM, VM, VM],
        out_specs=VM,
        out_shape=jax.ShapeDtypeStruct((TALL, C), F32),
        scratch_shapes=[
            pltpu.VMEM((8 * CAP, C), F32),
            pltpu.VMEM((3 * HEADS * HP, WIN), BF),
            pltpu.VMEM((HEADS * HP, WIN), BF),
            pltpu.SemaphoreType.DMA(()),
        ],
        compiler_params=params(),
    )(spots, own, slabs, g1, qkvt, owt, g2, w1t, w2t)


def back_kernel(spots_ref, done_ref, out_ref, rows, send, send_sem, recv_sem):
    near = neighbours()
    barrier = greet(near)
    meet(barrier, near)
    half = CAP // 2

    def gather(k, first, last):
        def block(b, carry):
            at = pl.multiple_of(b * 16, 16)
            got = [done_ref[pl.ds(spots_ref[k * SPOT_STRIDE + at + u], 1), :] for u in range(16)]
            rows[pl.ds(at, 16), :] = jnp.concatenate(got, 0)
            return carry

        lax.fori_loop(first, last, block, 0)

    def start(k):
        @pl.when(near[k][0])
        def _():
            push(k, near, send.at[k], out_ref.at[7 - k], send_sem, recv_sem).start()

    previous = None
    for k in SEND_ORDER:
        @pl.when(near[k][0])
        def _():
            gather(k, 0, 4)

        if previous is not None:
            start(previous)

        @pl.when(near[k][0])
        def _():
            gather(k, 4, CAP // 16)
            send[k, 0:CAP, :] = rows[:, 0:128].astype(BF)
            send[k, CAP:SLAB, :] = jnp.concatenate(
                [rows[0:half, 128:C], rows[half:CAP, 128:C]], 1
            ).astype(BF)

        previous = k
    start(previous)

    for k in SEND_ORDER:
        @pl.when(near[k][0])
        def _():
            push(k, near, send.at[k], out_ref.at[7 - k], send_sem, recv_sem).wait_send()
            push(7 - k, near, send.at[k], out_ref.at[k], send_sem, recv_sem).wait_recv()


def back(spots, done):
    return pl.pallas_call(
        back_kernel,
        name="back",
        in_specs=[SM, VM],
        out_specs=ANY,
        out_shape=jax.ShapeDtypeStruct((8, SLAB, 128), BF),
        scratch_shapes=[
            pltpu.VMEM((CAP, C), F32),
            pltpu.VMEM((8, SLAB, 128), BF),
            pltpu.SemaphoreType.DMA((8,)),
            pltpu.SemaphoreType.DMA((8,)),
        ],
        compiler_params=params(collective_id=2, has_side_effects=True),
    )(spots, done)


def collect_kernel(fetch_ref, done_ref, slab_ref, out_ref, table, rows, load_sem):
    home = pltpu.make_async_copy(done_ref.at[0:PTS, :], table.at[0:PTS, :], load_sem)
    home.start()
    near = neighbours()
    for k in range(8):
        @pl.when(near[k][0])
        def _():
            unpack(slab_ref[k], table, PTS + k * CAP)
    home.wait()

    def tile(i, carry):
        def block(b, inner):
            at = pl.multiple_of(b * 16, 16)
            got = [table[pl.ds(fetch_ref[i * 128 + at + u], 1), :] for u in range(16)]
            rows[pl.ds(at, 16), :] = jnp.concatenate(got, 0)
            return inner

        lax.fori_loop(0, 8, block, 0)
        out_ref[:, pl.ds(pl.multiple_of(i * 128, 128), 128)] = rows[...].T.astype(BF)
        return carry

    lax.fori_loop(0, PTS // 128, tile, 0)


def collect(fetch, done, slabs):
    return pl.pallas_call(
        collect_kernel,
        name="collect",
        in_specs=[SM, ANY, VM],
        out_specs=VM,
        out_shape=jax.ShapeDtypeStruct((C, PTS), BF),
        scratch_shapes=[
            pltpu.VMEM((PTS + 8 * CAP, C), F32),
            pltpu.VMEM((128, C), F32),
            pltpu.SemaphoreType.DMA(()),
        ],
        compiler_params=params(),
    )(fetch, done, slabs)


def on_device(
    feats, conv_weight, tap_index, halo_rows, hilbert_pos,
    ln1_gain, qkv_weight, out_weight, ln2_gain, mlp_in, mlp_out,
):
    feats_t = feats.T
    tap_t = tap_index.T
    fetch, sidx, spot, groups, hidx, cwt, qkvt, owt, g1, g2, w1t = prep(
        hilbert_pos.reshape(32, 128), tap_t, conv_weight.reshape(TAPS * C, C),
        halo_rows.reshape(32, 128), qkv_weight, out_weight,
        ln1_gain.reshape(1, C), ln2_gain.reshape(1, C), mlp_in,
    )
    fetch, sidx, spot, hidx = (a.reshape(PTS) for a in (fetch, sidx, spot, hidx))
    halo = halo_exchange(hidx, feats_t)
    own, slabs, spots = conv(groups, fetch, sidx, spot, tap_t, cwt, feats_t, halo)
    slabs, spots = deal(slabs, spots)
    done = windows(spots, own, slabs, g1, qkvt, owt, g2, w1t, mlp_out.T)
    arrived = back(spots, done)
    return collect(fetch, done, arrived).T


def solution(mesh):
    rows = P(("gx", "gy"), None)
    placed = (rows, P(), rows, P(("gx", "gy"), None, None), P(("gx", "gy"))) + (P(),) * 6
    return jax.shard_map(
        on_device, mesh=mesh, in_specs=placed, out_specs=rows, check_vma=False
    )
```

```python
import functools
import math

import jax
import jax.numpy as jnp
from jax import lax
from jax.experimental import pallas as pl
from jax.experimental.pallas import tpu as pltpu
from jax.sharding import PartitionSpec as P

BF = jnp.bfloat16
F32 = jnp.float32
I32 = jnp.int32
MESH = pl.DeviceIdType.MESH

C = 192
HEADS = 8
HD = 24
HP = 32
WIN = 1024
TAPS = 27
PTS = 4096
HB = 512
CAP = PTS // 16
GROUP = 128
SLOTS = PTS + 8 * CAP
ROWS = C + 16
VMEM_LIMIT = 60 * 1024 * 1024
SCALE = 1.0 / math.sqrt(HD) * math.log2(math.e)
SAFE = 80.0


def params(**kw):
    return pltpu.CompilerParams(vmem_limit_bytes=VMEM_LIMIT, **kw)


VM = pl.BlockSpec(memory_space=pltpu.VMEM)
SM = pl.BlockSpec(memory_space=pltpu.SMEM)
ANY = pl.BlockSpec(memory_space=pl.ANY)


def neighbour(k):
    j = k + k // 4
    x = lax.axis_index("gx") + j // 3 - 1
    y = lax.axis_index("gy") + j % 3 - 1
    inside = (x >= 0) & (x < lax.axis_size("gx")) & (y >= 0) & (y < lax.axis_size("gy"))
    return inside, x, y


def in_turn(i):
    return i + jnp.minimum(i, 1) - 3 * (i // 3)


def greet():
    barrier = pltpu.get_barrier_semaphore()
    count = jnp.int32(0)
    for k in range(8):
        inside, x, y = neighbour(k)
        count = count + inside.astype(I32)

        @pl.when(inside)
        def _():
            pl.semaphore_signal(barrier, inc=1, device_id=(x, y), device_id_type=MESH)

    return barrier, count


def push(k, src, dst, send_sem, recv_sem):
    _, x, y = neighbour(k)
    return pltpu.make_async_remote_copy(
        src_ref=src, dst_ref=dst, send_sem=send_sem.at[k], recv_sem=recv_sem.at[7 - k],
        device_id=(x, y), device_id_type=MESH,
    )


def each(body):
    def step(k, carry):
        body(k)
        return carry

    lax.fori_loop(0, 8, step, 0)


def index_row(ref, first, count):
    return jnp.concatenate([ref[pl.ds(first + u, 1), :] for u in range(count)], 1)


def select_columns(index, onehot):
    depth, width = onehot.shape
    for s in range(0, depth, 256):
        place = lax.broadcasted_iota(I32, (256, width), 0) + s
        onehot[s : s + 256, :] = jnp.where(place == index, 1.0, 0.0).astype(BF)


def prepare_indices(hp_ref, tap_ref, fetch_ref, own_ref, away_ref, spot_ref, group_ref, blank_ref):
    ix = lax.axis_index("gx")
    iy = lax.axis_index("gy")
    ny = lax.axis_size("gy")
    hp = hp_ref[...]
    target = hp // PTS
    local = hp - target * PTS
    step_x = target // ny - ix
    step_y = target % ny - iy
    code = 3 * (step_x + 1) + (step_y + 1)
    r128 = lax.broadcasted_iota(I32, (128, 128), 0)
    c128 = lax.broadcasted_iota(I32, (128, 128), 1)
    tri = (r128 < c128).astype(F32).astype(BF)
    r32 = lax.broadcasted_iota(I32, (32, 32), 0)
    c32 = lax.broadcasted_iota(I32, (32, 32), 1)
    low = (c32 < r32).astype(F32).astype(BF)
    before = jnp.zeros((32, 128), F32)
    for c in range(9):
        if c == 4:
            continue
        m = (code == c).astype(F32)
        mb = m.astype(BF)
        within = jnp.dot(mb, tri, preferred_element_type=F32)
        above = jnp.sum(jnp.dot(low, mb, preferred_element_type=F32), 1, keepdims=True)
        before = before + m * (within + above)
    away = (code - (code > 4).astype(I32)) * CAP + before.astype(I32)
    own = code == 4
    fetch_ref[...] = jnp.where(own, local, PTS + away)
    own_ref[...] = jnp.where(own, local, -1)
    away_ref[...] = jnp.where(own, -1, away)
    spot_ref[...] = local
    blank_ref[...] = jnp.full_like(blank_ref, -1)
    lane = lax.broadcasted_iota(I32, (TAPS, 128), 1)
    groups = jnp.zeros((TAPS, 128), I32)
    for i in range(PTS // 128):
        top = jnp.max(tap_ref[:, i * 128 : (i + 1) * 128], 1, keepdims=True)
        groups = jnp.where(lane == i, jnp.maximum(top, 0) // 128, groups)
    group_ref[...] = groups


def prepare_weights(
    cw_ref, qkvw_ref, ow_ref, g1_ref, g2_ref, w1_ref, cwt_ref, qkvt_ref, owt_ref, g1c_ref, g2c_ref, w1t_ref, pad
):
    for i in range(0, TAPS * C, 384):
        size = min(384, TAPS * C - i)
        cwt_ref[:, i : i + size] = cw_ref[i : i + size, :].astype(F32).T.astype(BF)
    wide = qkvw_ref[...].astype(F32).T
    pad[...] = jnp.zeros_like(pad)
    for j in range(3 * HEADS):
        pad[j * HP : j * HP + HD, :] = wide[j * HD : (j + 1) * HD, :]
    qkvt_ref[...] = pad[...].astype(BF)
    ow = ow_ref[...].astype(F32)
    for j in range(HEADS):
        pad[j * HP : j * HP + HD, :] = ow[j * HD : (j + 1) * HD, :]
    owt_ref[...] = pad[0 : HEADS * HP, :].T.astype(BF)
    g1c_ref[...] = jnp.broadcast_to(g1_ref[...], (128, C)).T
    g2c_ref[...] = jnp.broadcast_to(g2_ref[...], (128, C)).T
    w1t_ref[...] = w1_ref[...].astype(F32).T.astype(BF)


def halo_kernel(
    halo_ref, feats_ref, hp_ref, tap_ref, cw_ref, qkvw_ref, ow_ref, g1_ref, g2_ref, w1_ref,
    out_ref, fetch_ref, own_ref, away_ref, spot_ref, group_ref, blank_ref,
    cwt_ref, qkvt_ref, owt_ref, g1c_ref, g2c_ref, w1t_ref,
    onehot_a, onehot_b, send, zeros, pad, send_sem, recv_sem, zero_sem,
):
    barrier, count = greet()
    zeros[...] = jnp.zeros_like(zeros)

    def start(k):
        inside = neighbour(k)[0]

        @pl.when(inside)
        def _():
            push(k, send.at[k], out_ref.at[7 - k], send_sem, recv_sem).start()

        @pl.when(jnp.logical_not(inside))
        def _():
            pltpu.make_async_copy(zeros, out_ref.at[k], zero_sem.at[k]).start()

    pl.semaphore_wait(barrier, count)

    def pair(i, carry):
        k = in_turn(i)
        select_columns(halo_ref[pl.ds(k, 1), :], onehot_a)
        select_columns(halo_ref[pl.ds(7 - k, 1), :], onehot_b)

        @pl.when(i > 0)
        def _():
            start(7 - in_turn(i - 1))

        send[k] = jnp.dot(feats_ref[...], onehot_a[...], preferred_element_type=F32).astype(BF)
        send[7 - k] = jnp.dot(feats_ref[...], onehot_b[...], preferred_element_type=F32).astype(BF)
        start(k)
        return carry

    lax.fori_loop(0, 4, pair, 0)
    prepare_indices(hp_ref, tap_ref, fetch_ref, own_ref, away_ref, spot_ref, group_ref, blank_ref)
    start(7 - in_turn(3))
    prepare_weights(
        cw_ref, qkvw_ref, ow_ref, g1_ref, g2_ref, w1_ref,
        cwt_ref, qkvt_ref, owt_ref, g1c_ref, g2c_ref, w1t_ref, pad,
    )

    def finish(k):
        inside = neighbour(k)[0]

        @pl.when(inside)
        def _():
            push(k, send.at[k], out_ref.at[7 - k], send_sem, recv_sem).wait_send()
            push(7 - k, send.at[k], out_ref.at[k], send_sem, recv_sem).wait_recv()

        @pl.when(jnp.logical_not(inside))
        def _():
            pltpu.make_async_copy(zeros, out_ref.at[k], zero_sem.at[k]).wait()

    each(finish)


def halo_exchange(halo, feats_t, hp, tap_t, cw, qkvw, ow, g1, g2, w1):
    sd = jax.ShapeDtypeStruct
    return pl.pallas_call(
        halo_kernel,
        name="halo_exchange",
        in_specs=[VM] * 10,
        out_specs=[ANY] + [VM] * 12,
        out_shape=[
            sd((8, C, HB), BF),
            sd((32, 128), I32), sd((32, 128), I32), sd((32, 128), I32), sd((32, 128), I32),
            sd((TAPS, 128), I32), sd((SLOTS // 128, 128), I32),
            sd((C, TAPS * C), BF), sd((3 * HEADS * HP, C), BF), sd((C, HEADS * HP), BF),
            sd((C, 128), F32), sd((C, 128), F32), sd((4 * C, C), BF),
        ],
        scratch_shapes=[
            pltpu.VMEM((PTS, HB), BF),
            pltpu.VMEM((PTS, HB), BF),
            pltpu.VMEM((8, C, HB), BF),
            pltpu.VMEM((C, HB), BF),
            pltpu.VMEM((3 * HEADS * HP, C), F32),
            pltpu.SemaphoreType.DMA((8,)),
            pltpu.SemaphoreType.DMA((8,)),
            pltpu.SemaphoreType.DMA((8,)),
        ],
        compiler_params=params(collective_id=0, has_side_effects=True),
    )(halo, feats_t, hp, tap_t, cw, qkvw, ow, g1, g2, w1)


STEP = 4
CONV_STEPS = PTS // (128 * STEP)


def conv_kernel(
    group_ref, fetch_ref, spot_ref, tap_ref, cwt_ref, feats_ref, halo_ref, blank_ref,
    out_ref, source_ref, lookup, gathered, load_sem,
):
    i = pl.program_id(0)

    @pl.when(i == 0)
    def _():
        copies = [
            pltpu.make_async_copy(blank_ref, source_ref, load_sem.at[9]),
            pltpu.make_async_copy(feats_ref, lookup.at[:, 0:PTS], load_sem.at[8]),
        ]
        for k in range(8):
            at = PTS + k * HB
            copies.append(
                pltpu.make_async_copy(halo_ref.at[k], lookup.at[:, at : at + HB], load_sem.at[k])
            )
        for copy in copies:
            copy.start()
        for copy in copies:
            copy.wait()

    for n in range(STEP):
        def tap(t, carry):
            start = pl.multiple_of(group_ref[t, i * STEP + n] * 128, 128)
            source = lookup[:, pl.ds(start, 128)].astype(F32)
            index = jnp.broadcast_to(tap_ref[pl.ds(t, 1), n * 128 : (n + 1) * 128], (C, 128))
            taken = jnp.take_along_axis(source, index & 127, axis=1)
            taken = jnp.where(index >= 0, taken, 0.0)
            gathered[pl.ds(pl.multiple_of(t * C, C), C), n * 128 : (n + 1) * 128] = taken.astype(BF)
            return carry

        lax.fori_loop(0, TAPS, tap, 0, unroll=True)

    def note(b, carry):
        for u in range(32):
            p = i * (128 * STEP) + b * 32 + u
            source_ref[fetch_ref[p]] = p
        return carry

    lax.fori_loop(0, 4 * STEP, note, 0)
    conv = jnp.dot(cwt_ref[...], gathered[...], preferred_element_type=F32)
    here = lookup[:, pl.ds(pl.multiple_of(i * (128 * STEP), 128), 128 * STEP)].astype(F32)
    out_ref[0:C, :] = (here + conv).astype(BF)
    spot = index_row(spot_ref, 0, STEP) + 1
    number = lax.broadcasted_iota(I32, (ROWS - C, 128 * STEP), 0)
    digits = jnp.where(number == 0, spot // 64, jnp.where(number == 1, spot % 64, 0))
    out_ref[C:ROWS, :] = digits.astype(F32).astype(BF)


def conv(groups, fetch, spot, tap_t, cwt, feats_t, halo, blank):
    sd = jax.ShapeDtypeStruct
    return pl.pallas_call(
        conv_kernel,
        name="conv",
        grid=(CONV_STEPS,),
        in_specs=[
            SM, SM,
            pl.BlockSpec((None, STEP, 128), lambda i: (i, 0, 0)),
            pl.BlockSpec((TAPS, 128 * STEP), lambda i: (0, i)),
            pl.BlockSpec((C, TAPS * C), lambda i: (0, 0), pipeline_mode=pl.Buffered(1)),
            ANY, ANY, ANY,
        ],
        out_specs=[pl.BlockSpec((ROWS, 128 * STEP), lambda i: (0, i)), SM],
        out_shape=[sd((ROWS, PTS), BF), sd((SLOTS,), I32)],
        scratch_shapes=[
            pltpu.VMEM((C, PTS + 8 * HB), BF),
            pltpu.VMEM((TAPS * C, 128 * STEP), BF),
            pltpu.SemaphoreType.DMA((10,)),
        ],
        compiler_params=params(dimension_semantics=("arbitrary",)),
    )(groups, fetch, spot, tap_t, cwt, feats_t, halo, blank)


BLOCK = 512


def deal_kernel(updated_ref, source_ref, out_ref, spots_ref, onehot_a, onehot_b, send, recv, send_sem, recv_sem):
    barrier, count = greet()

    def blank(k):
        @pl.when(jnp.logical_not(neighbour(k)[0]))
        def _():
            recv[k] = jnp.zeros((ROWS, CAP), BF)

    each(blank)

    def start(k):
        @pl.when(neighbour(k)[0])
        def _():
            push(k, send.at[k], recv.at[7 - k], send_sem, recv_sem).start()

    pl.semaphore_wait(barrier, count)
    first = onehot_a.at[:, 0:CAP]
    second = onehot_b.at[:, 0:CAP]

    def pair(i, carry):
        k = in_turn(i)
        base = PTS // 128
        select_columns(index_row(source_ref, base + k * (CAP // 128), CAP // 128), first)
        select_columns(index_row(source_ref, base + (7 - k) * (CAP // 128), CAP // 128), second)

        @pl.when(i > 0)
        def _():
            start(7 - in_turn(i - 1))

        send[k] = jnp.dot(updated_ref[...], first[...], preferred_element_type=F32).astype(BF)
        send[7 - k] = jnp.dot(updated_ref[...], second[...], preferred_element_type=F32).astype(BF)
        start(k)
        return carry

    lax.fori_loop(0, 4, pair, 0)

    def stay(n, carry):
        select_columns(index_row(source_ref, n * (BLOCK // 128), BLOCK // 128), onehot_a)

        @pl.when(n == 0)
        def _():
            start(7 - in_turn(3))

        taken = jnp.dot(updated_ref[0:C, :], onehot_a[...], preferred_element_type=F32)
        out_ref[:, pl.ds(pl.multiple_of(n * BLOCK, BLOCK), BLOCK)] = taken.astype(BF)
        return carry

    lax.fori_loop(0, PTS // BLOCK, stay, 0)

    def finish(k):
        @pl.when(neighbour(k)[0])
        def _():
            push(k, send.at[k], recv.at[7 - k], send_sem, recv_sem).wait_send()
            push(7 - k, send.at[k], recv.at[k], send_sem, recv_sem).wait_recv()

    each(finish)

    for k in range(8):
        digits = recv[k, C:ROWS, :].astype(F32)
        spots_ref[k : k + 1, :] = (digits[0:1, :] * 64.0 + digits[1:2, :] - 1.0).astype(I32)

    def arrive(n, carry):
        total = jnp.zeros((C, BLOCK), F32)
        at = pl.multiple_of(n * BLOCK, BLOCK)
        place = lax.broadcasted_iota(I32, (BLOCK, CAP), 0) + at
        for k in range(8):
            chosen = jnp.where(place == spots_ref[k : k + 1, :], 1.0, 0.0).astype(BF)
            total = total + lax.dot_general(
                recv[k, 0:C, :], chosen, (((1,), (1,)), ((), ())), preferred_element_type=F32
            )
        here = out_ref[:, pl.ds(at, BLOCK)].astype(F32) + total
        out_ref[:, pl.ds(at, BLOCK)] = here.astype(BF)
        return carry

    lax.fori_loop(0, PTS // BLOCK, arrive, 0)


def deal(updated, source):
    sd = jax.ShapeDtypeStruct
    return pl.pallas_call(
        deal_kernel,
        name="deal",
        in_specs=[VM, VM],
        out_specs=[VM, VM],
        out_shape=[sd((C, PTS), BF), sd((8, CAP), I32)],
        scratch_shapes=[
            pltpu.VMEM((PTS, BLOCK), BF),
            pltpu.VMEM((PTS, BLOCK), BF),
            pltpu.VMEM((8, ROWS, CAP), BF),
            pltpu.VMEM((8, ROWS, CAP), BF),
            pltpu.SemaphoreType.DMA((8,)),
            pltpu.SemaphoreType.DMA((8,)),
        ],
        compiler_params=params(collective_id=1, has_side_effects=True),
    )(updated, source)


def norm_columns(values, gain):
    average = jnp.sum(values, 0, keepdims=True) * (1.0 / C)
    centred = values - average
    variance = jnp.sum(centred * centred, 0, keepdims=True) * (1.0 / C)
    return (centred * lax.rsqrt(variance + 1e-05) * gain).astype(BF)


def window_kernel(
    in_ref, g1_ref, qkvt_ref, owt_ref, g2_ref, w1t_ref, w2t_ref, out_ref, packed, attended
):
    def window(w, carry):
        base = pl.multiple_of(w * WIN, WIN)
        x = in_ref[:, pl.ds(base, WIN)].astype(F32)
        normed = norm_columns(x, g1_ref[:, 0:1])
        wide = HEADS * HP
        queries = jnp.dot(qkvt_ref[0:wide, :], normed, preferred_element_type=F32) * SCALE
        packed[0:wide, :] = queries.astype(BF)
        packed[wide : 3 * wide, :] = jnp.dot(
            qkvt_ref[wide : 3 * wide, :], normed, preferred_element_type=F32
        ).astype(BF)
        largest_q = jnp.zeros((1, WIN), F32)
        largest_k = jnp.zeros((1, WIN), F32)
        for h in range(HEADS):
            q = packed[h * HP : (h + 1) * HP, :].astype(F32)
            key = packed[wide + h * HP : wide + (h + 1) * HP, :].astype(F32)
            largest_q = jnp.maximum(largest_q, jnp.sum(q * q, 0, keepdims=True))
            largest_k = jnp.maximum(largest_k, jnp.sum(key * key, 0, keepdims=True))
        safe = jnp.max(largest_q) * jnp.max(largest_k) <= SAFE * SAFE

        def heads(shifted):
            def head(h, inner):
                off = pl.multiple_of(h * HP, HP)
                q = packed[pl.ds(off, HP), :]
                key = packed[pl.ds(wide + off, HP), :]
                value = packed[pl.ds(2 * wide + off, HP), :]
                number = lax.broadcasted_iota(I32, (HP, WIN), 0)
                value = jnp.where(number == HD, jnp.ones_like(value), value)
                scores = lax.dot_general(
                    key, q, (((0,), (0,)), ((), ())), preferred_element_type=F32
                )
                if shifted:
                    scores = scores - jnp.max(scores, 0, keepdims=True)
                probs = jnp.exp2(scores).astype(BF)
                mixed = jnp.dot(value, probs, preferred_element_type=F32)
                attended[pl.ds(off, HP), :] = (mixed / mixed[HD : HD + 1, :]).astype(BF)
                return inner

            lax.fori_loop(0, HEADS, head, 0, unroll=1 if shifted else 2)

        @pl.when(safe)
        def _():
            heads(False)

        @pl.when(jnp.logical_not(safe))
        def _():
            heads(True)

        residual = x + jnp.dot(owt_ref[...], attended[...], preferred_element_type=F32)
        residual = residual.astype(BF).astype(F32)
        normed_two = norm_columns(residual, g2_ref[:, 0:1])
        hidden = jnp.dot(w1t_ref[...], normed_two, preferred_element_type=F32)
        hidden = 0.5 * hidden * (1.0 + lax.erf(hidden * (2.0**-0.5)))
        processed = residual + jnp.dot(w2t_ref[...], hidden.astype(BF), preferred_element_type=F32)
        out_ref[:, pl.ds(base, WIN)] = processed.astype(BF)
        return carry

    lax.fori_loop(0, PTS // WIN, window, 0)


def windows(ordered, g1, qkvt, owt, g2, w1t, w2t):
    return pl.pallas_call(
        window_kernel,
        name="windows",
        in_specs=[VM] * 7,
        out_specs=VM,
        out_shape=jax.ShapeDtypeStruct((C, PTS), BF),
        scratch_shapes=[
            pltpu.VMEM((3 * HEADS * HP, WIN), BF),
            pltpu.VMEM((HEADS * HP, WIN), BF),
        ],
        compiler_params=params(),
    )(ordered, g1, qkvt, owt, g2, w1t, w2t)


def back_kernel(done_ref, spots_ref, own_ref, away_ref, out_ref, onehot_a, onehot_b, send, recv, send_sem, recv_sem):
    barrier, count = greet()

    def landing(k):
        return recv.at[:, pl.ds(pl.multiple_of(k * CAP, CAP), CAP)]

    def blank(k):
        @pl.when(jnp.logical_not(neighbour(k)[0]))
        def _():
            recv[:, pl.ds(pl.multiple_of(k * CAP, CAP), CAP)] = jnp.zeros((C, CAP), BF)

    each(blank)

    def start(k):
        @pl.when(neighbour(k)[0])
        def _():
            push(k, send.at[k], landing(7 - k), send_sem, recv_sem).start()

    pl.semaphore_wait(barrier, count)
    first = onehot_a.at[:, 0:CAP]
    second = onehot_b.at[:, 0:CAP]

    def pair(i, carry):
        k = in_turn(i)
        select_columns(spots_ref[pl.ds(k, 1), :], first)
        select_columns(spots_ref[pl.ds(7 - k, 1), :], second)

        @pl.when(i > 0)
        def _():
            start(7 - in_turn(i - 1))

        send[k] = jnp.dot(done_ref[...], first[...], preferred_element_type=F32).astype(BF)
        send[7 - k] = jnp.dot(done_ref[...], second[...], preferred_element_type=F32).astype(BF)
        start(k)
        return carry

    lax.fori_loop(0, 4, pair, 0)

    def stay(n, carry):
        select_columns(index_row(own_ref, n * (BLOCK // 128), BLOCK // 128), onehot_a)

        @pl.when(n == 0)
        def _():
            start(7 - in_turn(3))

        taken = jnp.dot(done_ref[...], onehot_a[...], preferred_element_type=F32)
        out_ref[:, pl.ds(pl.multiple_of(n * BLOCK, BLOCK), BLOCK)] = taken.astype(BF)
        return carry

    lax.fori_loop(0, PTS // BLOCK, stay, 0)

    def finish(k):
        @pl.when(neighbour(k)[0])
        def _():
            push(k, send.at[k], landing(7 - k), send_sem, recv_sem).wait_send()
            push(7 - k, send.at[k], landing(k), send_sem, recv_sem).wait_recv()

    each(finish)
    depth = 8 * CAP

    def returned(n, onehot):
        select_columns(index_row(away_ref, n * (BLOCK // 128), BLOCK // 128), onehot.at[0:depth, :])

    def add(n, onehot):
        taken = jnp.dot(recv[...], onehot[0:depth, :], preferred_element_type=F32)
        at = pl.multiple_of(n * BLOCK, BLOCK)
        here = out_ref[:, pl.ds(at, BLOCK)].astype(F32) + taken
        out_ref[:, pl.ds(at, BLOCK)] = here.astype(BF)

    def last(m, carry):
        returned(2 * m, onehot_a)
        returned(2 * m + 1, onehot_b)
        add(2 * m, onehot_a)
        add(2 * m + 1, onehot_b)
        return carry

    lax.fori_loop(0, PTS // BLOCK // 2, last, 0)


def back(done, spots, own, away):
    return pl.pallas_call(
        back_kernel,
        name="back",
        in_specs=[VM] * 4,
        out_specs=VM,
        out_shape=jax.ShapeDtypeStruct((C, PTS), BF),
        scratch_shapes=[
            pltpu.VMEM((PTS, BLOCK), BF),
            pltpu.VMEM((PTS, BLOCK), BF),
            pltpu.VMEM((8, C, CAP), BF),
            pltpu.VMEM((C, 8 * CAP), BF),
            pltpu.SemaphoreType.DMA((8,)),
            pltpu.SemaphoreType.DMA((8,)),
        ],
        compiler_params=params(collective_id=2, has_side_effects=True),
    )(done, spots, own, away)


def on_device(
    feats, conv_weight, tap_index, halo_rows, hilbert_pos,
    ln1_gain, qkv_weight, out_weight, ln2_gain, mlp_in, mlp_out,
):
    feats_t = feats.T
    tap_t = tap_index.T
    halo, fetch, own, away, spot, groups, blank, cwt, qkvt, owt, g1, g2, w1t = halo_exchange(
        halo_rows[0], feats_t, hilbert_pos.reshape(32, 128), tap_t,
        conv_weight.reshape(TAPS * C, C), qkv_weight, out_weight,
        ln1_gain.reshape(1, C), ln2_gain.reshape(1, C), mlp_in,
    )
    updated, source = conv(
        groups, fetch.reshape(PTS), spot.reshape(CONV_STEPS, STEP, 128), tap_t, cwt, feats_t, halo,
        blank.reshape(SLOTS),
    )
    ordered, spots = deal(updated, source.reshape(SLOTS // 128, 128))
    done = windows(ordered, g1, qkvt, owt, g2, w1t, mlp_out.T)
    return back(done, spots, own, away).T


def solution(mesh):
    rows = P(("gx", "gy"), None)
    placed = (rows, P(), rows, P(("gx", "gy"), None, None), P(("gx", "gy"))) + (P(),) * 6
    return jax.shard_map(
        on_device, mesh=mesh, in_specs=placed, out_specs=rows, check_vma=False
    )
```

```python
import functools
import math

import jax
import jax.numpy as jnp
from jax import lax
from jax.experimental import pallas as pl
from jax.experimental.pallas import tpu as pltpu
from jax.sharding import PartitionSpec as P

BF = jnp.bfloat16
F32 = jnp.float32
I32 = jnp.int32
MESH = pl.DeviceIdType.MESH

C = 192
HEADS = 8
HD = 24
HP = 32
WIN = 1024
TAPS = 27
PTS = 4096
HB = 512
CAP = PTS // 16
GROUP = 128
SLOTS = PTS + 8 * CAP
ROWS = C + 16
VMEM_LIMIT = 60 * 1024 * 1024
SCALE = 1.0 / math.sqrt(HD) * math.log2(math.e)
SAFE = 80.0


def params(**kw):
    return pltpu.CompilerParams(vmem_limit_bytes=VMEM_LIMIT, **kw)


VM = pl.BlockSpec(memory_space=pltpu.VMEM)
SM = pl.BlockSpec(memory_space=pltpu.SMEM)
ANY = pl.BlockSpec(memory_space=pl.ANY)


def neighbour(k):
    j = k + k // 4
    x = lax.axis_index("gx") + j // 3 - 1
    y = lax.axis_index("gy") + j % 3 - 1
    inside = (x >= 0) & (x < lax.axis_size("gx")) & (y >= 0) & (y < lax.axis_size("gy"))
    return inside, x, y


def in_turn(i):
    return i + jnp.minimum(i, 1) - 3 * (i // 3)


def greet():
    barrier = pltpu.get_barrier_semaphore()
    count = jnp.int32(0)
    for k in range(8):
        inside, x, y = neighbour(k)
        count = count + inside.astype(I32)

        @pl.when(inside)
        def _():
            pl.semaphore_signal(barrier, inc=1, device_id=(x, y), device_id_type=MESH)

    return barrier, count


def push(k, src, dst, send_sem, recv_sem):
    _, x, y = neighbour(k)
    return pltpu.make_async_remote_copy(
        src_ref=src, dst_ref=dst, send_sem=send_sem.at[k], recv_sem=recv_sem.at[7 - k],
        device_id=(x, y), device_id_type=MESH,
    )


def each(body):
    def step(k, carry):
        body(k)
        return carry

    lax.fori_loop(0, 8, step, 0)


def index_row(ref, first, count):
    return jnp.concatenate([ref[pl.ds(first + u, 1), :] for u in range(count)], 1)


def select_columns(index, onehot):
    depth, width = onehot.shape
    for s in range(0, depth, 256):
        place = lax.broadcasted_iota(I32, (256, width), 0) + s
        onehot[s : s + 256, :] = jnp.where(place == index, 1.0, 0.0).astype(BF)


def prepare_indices(hp_ref, tap_ref, fetch_ref, own_ref, away_ref, spot_ref, group_ref, blank_ref):
    ix = lax.axis_index("gx")
    iy = lax.axis_index("gy")
    ny = lax.axis_size("gy")
    hp = hp_ref[...]
    target = hp // PTS
    local = hp - target * PTS
    step_x = target // ny - ix
    step_y = target % ny - iy
    code = 3 * (step_x + 1) + (step_y + 1)
    r128 = lax.broadcasted_iota(I32, (128, 128), 0)
    c128 = lax.broadcasted_iota(I32, (128, 128), 1)
    tri = (r128 < c128).astype(F32).astype(BF)
    r32 = lax.broadcasted_iota(I32, (32, 32), 0)
    c32 = lax.broadcasted_iota(I32, (32, 32), 1)
    low = (c32 < r32).astype(F32).astype(BF)
    before = jnp.zeros((32, 128), F32)
    for c in range(9):
        if c == 4:
            continue
        m = (code == c).astype(F32)
        mb = m.astype(BF)
        within = jnp.dot(mb, tri, preferred_element_type=F32)
        above = jnp.sum(jnp.dot(low, mb, preferred_element_type=F32), 1, keepdims=True)
        before = before + m * (within + above)
    away = (code - (code > 4).astype(I32)) * CAP + before.astype(I32)
    own = code == 4
    fetch_ref[...] = jnp.where(own, local, PTS + away)
    own_ref[...] = jnp.where(own, local, -1)
    away_ref[...] = jnp.where(own, -1, away)
    spot_ref[...] = local
    blank_ref[...] = jnp.full_like(blank_ref, -1)
    lane = lax.broadcasted_iota(I32, (TAPS, 128), 1)
    groups = jnp.zeros((TAPS, 128), I32)
    for i in range(PTS // 128):
        top = jnp.max(tap_ref[:, i * 128 : (i + 1) * 128], 1, keepdims=True)
        groups = jnp.where(lane == i, jnp.maximum(top, 0) // 128, groups)
    group_ref[...] = groups


def prepare_weights(
    cw_ref, qkvw_ref, ow_ref, g1_ref, g2_ref, w1_ref, cwt_ref, qkvt_ref, owt_ref, g1c_ref, g2c_ref, w1t_ref, pad
):
    for i in range(0, TAPS * C, 384):
        size = min(384, TAPS * C - i)
        cwt_ref[:, i : i + size] = cw_ref[i : i + size, :].astype(F32).T.astype(BF)
    wide = qkvw_ref[...].astype(F32).T
    pad[...] = jnp.zeros_like(pad)
    for j in range(3 * HEADS):
        pad[j * HP : j * HP + HD, :] = wide[j * HD : (j + 1) * HD, :]
    qkvt_ref[...] = pad[...].astype(BF)
    ow = ow_ref[...].astype(F32)
    for j in range(HEADS):
        pad[j * HP : j * HP + HD, :] = ow[j * HD : (j + 1) * HD, :]
    owt_ref[...] = pad[0 : HEADS * HP, :].T.astype(BF)
    g1c_ref[...] = jnp.broadcast_to(g1_ref[...], (128, C)).T
    g2c_ref[...] = jnp.broadcast_to(g2_ref[...], (128, C)).T
    w1t_ref[...] = w1_ref[...].astype(F32).T.astype(BF)


def halo_kernel(
    halo_ref, feats_ref, hp_ref, tap_ref, cw_ref, qkvw_ref, ow_ref, g1_ref, g2_ref, w1_ref,
    out_ref, fetch_ref, own_ref, away_ref, spot_ref, group_ref, blank_ref,
    cwt_ref, qkvt_ref, owt_ref, g1c_ref, g2c_ref, w1t_ref,
    onehot_a, onehot_b, send, zeros, pad, send_sem, recv_sem, zero_sem,
):
    barrier, count = greet()
    zeros[...] = jnp.zeros_like(zeros)

    def start(k):
        inside = neighbour(k)[0]

        @pl.when(inside)
        def _():
            push(k, send.at[k], out_ref.at[7 - k], send_sem, recv_sem).start()

        @pl.when(jnp.logical_not(inside))
        def _():
            pltpu.make_async_copy(zeros, out_ref.at[k], zero_sem.at[k]).start()

    pl.semaphore_wait(barrier, count)

    def pair(i, carry):
        k = in_turn(i)
        select_columns(halo_ref[pl.ds(k, 1), :], onehot_a)
        select_columns(halo_ref[pl.ds(7 - k, 1), :], onehot_b)

        send[k] = jnp.dot(feats_ref[...], onehot_a[...], preferred_element_type=F32).astype(BF)
        send[7 - k] = jnp.dot(feats_ref[...], onehot_b[...], preferred_element_type=F32).astype(BF)
        start(k)
        start(7 - k)
        return carry

    lax.fori_loop(0, 4, pair, 0)
    prepare_indices(hp_ref, tap_ref, fetch_ref, own_ref, away_ref, spot_ref, group_ref, blank_ref)
    prepare_weights(
        cw_ref, qkvw_ref, ow_ref, g1_ref, g2_ref, w1_ref,
        cwt_ref, qkvt_ref, owt_ref, g1c_ref, g2c_ref, w1t_ref, pad,
    )

    def finish(k):
        inside = neighbour(k)[0]

        @pl.when(inside)
        def _():
            push(k, send.at[k], out_ref.at[7 - k], send_sem, recv_sem).wait_send()
            push(7 - k, send.at[k], out_ref.at[k], send_sem, recv_sem).wait_recv()

        @pl.when(jnp.logical_not(inside))
        def _():
            pltpu.make_async_copy(zeros, out_ref.at[k], zero_sem.at[k]).wait()

    each(finish)


def halo_exchange(halo, feats_t, hp, tap_t, cw, qkvw, ow, g1, g2, w1):
    sd = jax.ShapeDtypeStruct
    return pl.pallas_call(
        halo_kernel,
        name="halo_exchange",
        in_specs=[VM] * 10,
        out_specs=[ANY] + [VM] * 12,
        out_shape=[
            sd((8, C, HB), BF),
            sd((32, 128), I32), sd((32, 128), I32), sd((32, 128), I32), sd((32, 128), I32),
            sd((TAPS, 128), I32), sd((SLOTS // 128, 128), I32),
            sd((C, TAPS * C), BF), sd((3 * HEADS * HP, C), BF), sd((C, HEADS * HP), BF),
            sd((C, 128), F32), sd((C, 128), F32), sd((4 * C, C), BF),
        ],
        scratch_shapes=[
            pltpu.VMEM((PTS, HB), BF),
            pltpu.VMEM((PTS, HB), BF),
            pltpu.VMEM((8, C, HB), BF),
            pltpu.VMEM((C, HB), BF),
            pltpu.VMEM((3 * HEADS * HP, C), F32),
            pltpu.SemaphoreType.DMA((8,)),
            pltpu.SemaphoreType.DMA((8,)),
            pltpu.SemaphoreType.DMA((8,)),
        ],
        compiler_params=params(collective_id=0, has_side_effects=True),
    )(halo, feats_t, hp, tap_t, cw, qkvw, ow, g1, g2, w1)


STEP = 4
CONV_STEPS = PTS // (128 * STEP)


def conv_kernel(
    group_ref, fetch_ref, spot_ref, tap_ref, cwt_ref, feats_ref, halo_ref, blank_ref,
    out_ref, source_ref, lookup, gathered, load_sem,
):
    i = pl.program_id(0)

    @pl.when(i == 0)
    def _():
        copies = [
            pltpu.make_async_copy(blank_ref, source_ref, load_sem.at[9]),
            pltpu.make_async_copy(feats_ref, lookup.at[:, 0:PTS], load_sem.at[8]),
        ]
        for k in range(8):
            at = PTS + k * HB
            copies.append(
                pltpu.make_async_copy(halo_ref.at[k], lookup.at[:, at : at + HB], load_sem.at[k])
            )
        for copy in copies:
            copy.start()
        for copy in copies:
            copy.wait()

    for n in range(STEP):
        def tap(t, carry):
            start = pl.multiple_of(group_ref[t, i * STEP + n] * 128, 128)
            source = lookup[:, pl.ds(start, 128)].astype(F32)
            index = jnp.broadcast_to(tap_ref[pl.ds(t, 1), n * 128 : (n + 1) * 128], (C, 128))
            taken = jnp.take_along_axis(source, index & 127, axis=1)
            taken = jnp.where(index >= 0, taken, 0.0)
            gathered[pl.ds(pl.multiple_of(t * C, C), C), n * 128 : (n + 1) * 128] = taken.astype(BF)
            return carry

        lax.fori_loop(0, TAPS, tap, 0, unroll=True)

    def note(b, carry):
        for u in range(32):
            p = i * (128 * STEP) + b * 32 + u
            source_ref[fetch_ref[p]] = p
        return carry

    lax.fori_loop(0, 4 * STEP, note, 0)
    conv = jnp.dot(cwt_ref[...], gathered[...], preferred_element_type=F32)
    here = lookup[:, pl.ds(pl.multiple_of(i * (128 * STEP), 128), 128 * STEP)].astype(F32)
    out_ref[0:C, :] = (here + conv).astype(BF)
    spot = index_row(spot_ref, 0, STEP) + 1
    number = lax.broadcasted_iota(I32, (ROWS - C, 128 * STEP), 0)
    digits = jnp.where(number == 0, spot // 64, jnp.where(number == 1, spot % 64, 0))
    out_ref[C:ROWS, :] = digits.astype(F32).astype(BF)


def conv(groups, fetch, spot, tap_t, cwt, feats_t, halo, blank):
    sd = jax.ShapeDtypeStruct
    return pl.pallas_call(
        conv_kernel,
        name="conv",
        grid=(CONV_STEPS,),
        in_specs=[
            SM, SM,
            pl.BlockSpec((None, STEP, 128), lambda i: (i, 0, 0)),
            pl.BlockSpec((TAPS, 128 * STEP), lambda i: (0, i)),
            pl.BlockSpec((C, TAPS * C), lambda i: (0, 0), pipeline_mode=pl.Buffered(1)),
            ANY, ANY, ANY,
        ],
        out_specs=[pl.BlockSpec((ROWS, 128 * STEP), lambda i: (0, i)), SM],
        out_shape=[sd((ROWS, PTS), BF), sd((SLOTS,), I32)],
        scratch_shapes=[
            pltpu.VMEM((C, PTS + 8 * HB), BF),
            pltpu.VMEM((TAPS * C, 128 * STEP), BF),
            pltpu.SemaphoreType.DMA((10,)),
        ],
        compiler_params=params(dimension_semantics=("arbitrary",)),
    )(groups, fetch, spot, tap_t, cwt, feats_t, halo, blank)


BLOCK = 512


def deal_kernel(updated_ref, source_ref, out_ref, spots_ref, onehot_a, onehot_b, send, recv, send_sem, recv_sem):
    barrier, count = greet()

    def blank(k):
        @pl.when(jnp.logical_not(neighbour(k)[0]))
        def _():
            recv[k] = jnp.zeros((ROWS, CAP), BF)

    each(blank)

    def start(k):
        @pl.when(neighbour(k)[0])
        def _():
            push(k, send.at[k], recv.at[7 - k], send_sem, recv_sem).start()

    pl.semaphore_wait(barrier, count)
    first = onehot_a.at[:, 0:CAP]
    second = onehot_b.at[:, 0:CAP]

    def pair(i, carry):
        k = in_turn(i)
        base = PTS // 128
        select_columns(index_row(source_ref, base + k * (CAP // 128), CAP // 128), first)
        select_columns(index_row(source_ref, base + (7 - k) * (CAP // 128), CAP // 128), second)

        send[k] = jnp.dot(updated_ref[...], first[...], preferred_element_type=F32).astype(BF)
        send[7 - k] = jnp.dot(updated_ref[...], second[...], preferred_element_type=F32).astype(BF)
        start(k)
        start(7 - k)
        return carry

    lax.fori_loop(0, 4, pair, 0)

    def stay(n, carry):
        select_columns(index_row(source_ref, n * (BLOCK // 128), BLOCK // 128), onehot_a)

        taken = jnp.dot(updated_ref[0:C, :], onehot_a[...], preferred_element_type=F32)
        out_ref[:, pl.ds(pl.multiple_of(n * BLOCK, BLOCK), BLOCK)] = taken.astype(BF)
        return carry

    lax.fori_loop(0, PTS // BLOCK, stay, 0)

    def finish(k):
        @pl.when(neighbour(k)[0])
        def _():
            push(k, send.at[k], recv.at[7 - k], send_sem, recv_sem).wait_send()
            push(7 - k, send.at[k], recv.at[k], send_sem, recv_sem).wait_recv()

    each(finish)

    for k in range(8):
        digits = recv[k, C:ROWS, :].astype(F32)
        spots_ref[k : k + 1, :] = (digits[0:1, :] * 64.0 + digits[1:2, :] - 1.0).astype(I32)

    def arrive(n, carry):
        total = jnp.zeros((C, BLOCK), F32)
        at = pl.multiple_of(n * BLOCK, BLOCK)
        place = lax.broadcasted_iota(I32, (BLOCK, CAP), 0) + at
        for k in range(8):
            chosen = jnp.where(place == spots_ref[k : k + 1, :], 1.0, 0.0).astype(BF)
            total = total + lax.dot_general(
                recv[k, 0:C, :], chosen, (((1,), (1,)), ((), ())), preferred_element_type=F32
            )
        here = out_ref[:, pl.ds(at, BLOCK)].astype(F32) + total
        out_ref[:, pl.ds(at, BLOCK)] = here.astype(BF)
        return carry

    lax.fori_loop(0, PTS // BLOCK, arrive, 0)


def deal(updated, source):
    sd = jax.ShapeDtypeStruct
    return pl.pallas_call(
        deal_kernel,
        name="deal",
        in_specs=[VM, VM],
        out_specs=[VM, VM],
        out_shape=[sd((C, PTS), BF), sd((8, CAP), I32)],
        scratch_shapes=[
            pltpu.VMEM((PTS, BLOCK), BF),
            pltpu.VMEM((PTS, BLOCK), BF),
            pltpu.VMEM((8, ROWS, CAP), BF),
            pltpu.VMEM((8, ROWS, CAP), BF),
            pltpu.SemaphoreType.DMA((8,)),
            pltpu.SemaphoreType.DMA((8,)),
        ],
        compiler_params=params(collective_id=1, has_side_effects=True),
    )(updated, source)


def norm_columns(values, gain):
    average = jnp.sum(values, 0, keepdims=True) * (1.0 / C)
    centred = values - average
    variance = jnp.sum(centred * centred, 0, keepdims=True) * (1.0 / C)
    return (centred * lax.rsqrt(variance + 1e-05) * gain).astype(BF)


def window_kernel(
    in_ref, g1_ref, qkvt_ref, owt_ref, g2_ref, w1t_ref, w2t_ref, out_ref, packed, attended
):
    def window(w, carry):
        base = pl.multiple_of(w * WIN, WIN)
        x = in_ref[:, pl.ds(base, WIN)].astype(F32)
        normed = norm_columns(x, g1_ref[:, 0:1])
        wide = HEADS * HP
        queries = jnp.dot(qkvt_ref[0:wide, :], normed, preferred_element_type=F32) * SCALE
        packed[0:wide, :] = queries.astype(BF)
        packed[wide : 3 * wide, :] = jnp.dot(
            qkvt_ref[wide : 3 * wide, :], normed, preferred_element_type=F32
        ).astype(BF)
        largest_q = jnp.zeros((1, WIN), F32)
        largest_k = jnp.zeros((1, WIN), F32)
        for h in range(HEADS):
            q = packed[h * HP : (h + 1) * HP, :].astype(F32)
            key = packed[wide + h * HP : wide + (h + 1) * HP, :].astype(F32)
            largest_q = jnp.maximum(largest_q, jnp.sum(q * q, 0, keepdims=True))
            largest_k = jnp.maximum(largest_k, jnp.sum(key * key, 0, keepdims=True))
        safe = jnp.max(largest_q) * jnp.max(largest_k) <= SAFE * SAFE

        def heads(shifted):
            def head(h, inner):
                off = pl.multiple_of(h * HP, HP)
                q = packed[pl.ds(off, HP), :]
                key = packed[pl.ds(wide + off, HP), :]
                value = packed[pl.ds(2 * wide + off, HP), :]
                number = lax.broadcasted_iota(I32, (HP, WIN), 0)
                value = jnp.where(number == HD, jnp.ones_like(value), value)
                scores = lax.dot_general(
                    key, q, (((0,), (0,)), ((), ())), preferred_element_type=F32
                )
                if shifted:
                    scores = scores - jnp.max(scores, 0, keepdims=True)
                probs = jnp.exp2(scores).astype(BF)
                mixed = jnp.dot(value, probs, preferred_element_type=F32)
                attended[pl.ds(off, HP), :] = (mixed / mixed[HD : HD + 1, :]).astype(BF)
                return inner

            lax.fori_loop(0, HEADS, head, 0, unroll=1 if shifted else 4)

        @pl.when(safe)
        def _():
            heads(False)

        @pl.when(jnp.logical_not(safe))
        def _():
            heads(True)

        residual = x + jnp.dot(owt_ref[...], attended[...], preferred_element_type=F32)
        residual = residual.astype(BF).astype(F32)
        normed_two = norm_columns(residual, g2_ref[:, 0:1])
        hidden = jnp.dot(w1t_ref[...], normed_two, preferred_element_type=F32)
        hidden = 0.5 * hidden * (1.0 + lax.erf(hidden * (2.0**-0.5)))
        processed = residual + jnp.dot(w2t_ref[...], hidden.astype(BF), preferred_element_type=F32)
        out_ref[:, pl.ds(base, WIN)] = processed.astype(BF)
        return carry

    lax.fori_loop(0, PTS // WIN, window, 0)


def windows(ordered, g1, qkvt, owt, g2, w1t, w2t):
    return pl.pallas_call(
        window_kernel,
        name="windows",
        in_specs=[VM] * 7,
        out_specs=VM,
        out_shape=jax.ShapeDtypeStruct((C, PTS), BF),
        scratch_shapes=[
            pltpu.VMEM((3 * HEADS * HP, WIN), BF),
            pltpu.VMEM((HEADS * HP, WIN), BF),
        ],
        compiler_params=params(),
    )(ordered, g1, qkvt, owt, g2, w1t, w2t)


def back_kernel(done_ref, spots_ref, own_ref, away_ref, out_ref, onehot_a, onehot_b, send, recv, send_sem, recv_sem):
    barrier, count = greet()

    def landing(k):
        return recv.at[:, pl.ds(pl.multiple_of(k * CAP, CAP), CAP)]

    def blank(k):
        @pl.when(jnp.logical_not(neighbour(k)[0]))
        def _():
            recv[:, pl.ds(pl.multiple_of(k * CAP, CAP), CAP)] = jnp.zeros((C, CAP), BF)

    each(blank)

    def start(k):
        @pl.when(neighbour(k)[0])
        def _():
            push(k, send.at[k], landing(7 - k), send_sem, recv_sem).start()

    pl.semaphore_wait(barrier, count)
    first = onehot_a.at[:, 0:CAP]
    second = onehot_b.at[:, 0:CAP]

    def pair(i, carry):
        k = in_turn(i)
        select_columns(spots_ref[pl.ds(k, 1), :], first)
        select_columns(spots_ref[pl.ds(7 - k, 1), :], second)

        send[k] = jnp.dot(done_ref[...], first[...], preferred_element_type=F32).astype(BF)
        send[7 - k] = jnp.dot(done_ref[...], second[...], preferred_element_type=F32).astype(BF)
        start(k)
        start(7 - k)
        return carry

    lax.fori_loop(0, 4, pair, 0)

    def stay(n, carry):
        select_columns(index_row(own_ref, n * (BLOCK // 128), BLOCK // 128), onehot_a)

        taken = jnp.dot(done_ref[...], onehot_a[...], preferred_element_type=F32)
        out_ref[:, pl.ds(pl.multiple_of(n * BLOCK, BLOCK), BLOCK)] = taken.astype(BF)
        return carry

    lax.fori_loop(0, PTS // BLOCK, stay, 0)

    def finish(k):
        @pl.when(neighbour(k)[0])
        def _():
            push(k, send.at[k], landing(7 - k), send_sem, recv_sem).wait_send()
            push(7 - k, send.at[k], landing(k), send_sem, recv_sem).wait_recv()

    each(finish)
    depth = 8 * CAP

    def returned(n, onehot):
        select_columns(index_row(away_ref, n * (BLOCK // 128), BLOCK // 128), onehot.at[0:depth, :])

    def add(n, onehot):
        taken = jnp.dot(recv[...], onehot[0:depth, :], preferred_element_type=F32)
        at = pl.multiple_of(n * BLOCK, BLOCK)
        here = out_ref[:, pl.ds(at, BLOCK)].astype(F32) + taken
        out_ref[:, pl.ds(at, BLOCK)] = here.astype(BF)

    def last(m, carry):
        returned(2 * m, onehot_a)
        returned(2 * m + 1, onehot_b)
        add(2 * m, onehot_a)
        add(2 * m + 1, onehot_b)
        return carry

    lax.fori_loop(0, PTS // BLOCK // 2, last, 0)


def back(done, spots, own, away):
    return pl.pallas_call(
        back_kernel,
        name="back",
        in_specs=[VM] * 4,
        out_specs=VM,
        out_shape=jax.ShapeDtypeStruct((C, PTS), BF),
        scratch_shapes=[
            pltpu.VMEM((PTS, BLOCK), BF),
            pltpu.VMEM((PTS, BLOCK), BF),
            pltpu.VMEM((8, C, CAP), BF),
            pltpu.VMEM((C, 8 * CAP), BF),
            pltpu.SemaphoreType.DMA((8,)),
            pltpu.SemaphoreType.DMA((8,)),
        ],
        compiler_params=params(collective_id=2, has_side_effects=True),
    )(done, spots, own, away)


def on_device(
    feats, conv_weight, tap_index, halo_rows, hilbert_pos,
    ln1_gain, qkv_weight, out_weight, ln2_gain, mlp_in, mlp_out,
):
    feats_t = feats.T
    tap_t = tap_index.T
    halo, fetch, own, away, spot, groups, blank, cwt, qkvt, owt, g1, g2, w1t = halo_exchange(
        halo_rows[0], feats_t, hilbert_pos.reshape(32, 128), tap_t,
        conv_weight.reshape(TAPS * C, C), qkv_weight, out_weight,
        ln1_gain.reshape(1, C), ln2_gain.reshape(1, C), mlp_in,
    )
    updated, source = conv(
        groups, fetch.reshape(PTS), spot.reshape(CONV_STEPS, STEP, 128), tap_t, cwt, feats_t, halo,
        blank.reshape(SLOTS),
    )
    ordered, spots = deal(updated, source.reshape(SLOTS // 128, 128))
    done = windows(ordered, g1, qkvt, owt, g2, w1t, mlp_out.T)
    return back(done, spots, own, away).T


def solution(mesh):
    rows = P(("gx", "gy"), None)
    placed = (rows, P(), rows, P(("gx", "gy"), None, None), P(("gx", "gy"))) + (P(),) * 6
    return jax.shard_map(
        on_device, mesh=mesh, in_specs=placed, out_specs=rows, check_vma=False
    )
```

```python
import functools
import math

import jax
import jax.numpy as jnp
from jax import lax
from jax.experimental import pallas as pl
from jax.experimental.pallas import tpu as pltpu
from jax.sharding import PartitionSpec as P

BF = jnp.bfloat16
F32 = jnp.float32
I32 = jnp.int32
MESH = pl.DeviceIdType.MESH

C = 192
HEADS = 8
HD = 24
HP = 32
WIN = 1024
TAPS = 27
PTS = 4096
HB = 512
CAP = PTS // 16
GROUP = 128
SLOTS = PTS + 8 * CAP
ROWS = C + 16
VMEM_LIMIT = 60 * 1024 * 1024
SCALE = 1.0 / math.sqrt(HD) * math.log2(math.e)
SAFE = 80.0


def params(**kw):
    return pltpu.CompilerParams(vmem_limit_bytes=VMEM_LIMIT, **kw)


VM = pl.BlockSpec(memory_space=pltpu.VMEM)
SM = pl.BlockSpec(memory_space=pltpu.SMEM)
ANY = pl.BlockSpec(memory_space=pl.ANY)


def neighbour(k):
    j = k + k // 4
    x = lax.axis_index("gx") + j // 3 - 1
    y = lax.axis_index("gy") + j % 3 - 1
    inside = (x >= 0) & (x < lax.axis_size("gx")) & (y >= 0) & (y < lax.axis_size("gy"))
    return inside, x, y


def in_turn(i):
    return i + jnp.minimum(i, 1) - 3 * (i // 3)


def greet():
    barrier = pltpu.get_barrier_semaphore()
    count = jnp.int32(0)
    for k in range(8):
        inside, x, y = neighbour(k)
        count = count + inside.astype(I32)

        @pl.when(inside)
        def _():
            pl.semaphore_signal(barrier, inc=1, device_id=(x, y), device_id_type=MESH)

    return barrier, count


def push(k, src, dst, send_sem, recv_sem):
    _, x, y = neighbour(k)
    return pltpu.make_async_remote_copy(
        src_ref=src, dst_ref=dst, send_sem=send_sem.at[k], recv_sem=recv_sem.at[7 - k],
        device_id=(x, y), device_id_type=MESH,
    )


def each(body):
    def step(k, carry):
        body(k)
        return carry

    lax.fori_loop(0, 8, step, 0)


def index_row(ref, first, count):
    return jnp.concatenate([ref[pl.ds(first + u, 1), :] for u in range(count)], 1)


def select_columns(index, onehot):
    depth, width = onehot.shape
    for s in range(0, depth, 256):
        place = lax.broadcasted_iota(I32, (256, width), 0) + s
        onehot[s : s + 256, :] = jnp.where(place == index, 1.0, 0.0).astype(BF)


def prepare_indices(hp_ref, tap_ref, fetch_ref, own_ref, away_ref, spot_ref, group_ref, blank_ref):
    ix = lax.axis_index("gx")
    iy = lax.axis_index("gy")
    ny = lax.axis_size("gy")
    hp = hp_ref[...]
    target = hp // PTS
    local = hp - target * PTS
    step_x = target // ny - ix
    step_y = target % ny - iy
    code = 3 * (step_x + 1) + (step_y + 1)
    r128 = lax.broadcasted_iota(I32, (128, 128), 0)
    c128 = lax.broadcasted_iota(I32, (128, 128), 1)
    tri = (r128 < c128).astype(F32).astype(BF)
    r32 = lax.broadcasted_iota(I32, (32, 32), 0)
    c32 = lax.broadcasted_iota(I32, (32, 32), 1)
    low = (c32 < r32).astype(F32).astype(BF)
    before = jnp.zeros((32, 128), F32)
    for c in range(9):
        if c == 4:
            continue
        m = (code == c).astype(F32)
        mb = m.astype(BF)
        within = jnp.dot(mb, tri, preferred_element_type=F32)
        above = jnp.sum(jnp.dot(low, mb, preferred_element_type=F32), 1, keepdims=True)
        before = before + m * (within + above)
    away = (code - (code > 4).astype(I32)) * CAP + before.astype(I32)
    own = code == 4
    fetch_ref[...] = jnp.where(own, local, PTS + away)
    own_ref[...] = jnp.where(own, local, -1)
    away_ref[...] = jnp.where(own, -1, away)
    spot_ref[...] = local
    blank_ref[...] = jnp.full_like(blank_ref, -1)
    lane = lax.broadcasted_iota(I32, (TAPS, 128), 1)
    groups = jnp.zeros((TAPS, 128), I32)
    for i in range(PTS // 128):
        top = jnp.max(tap_ref[:, i * 128 : (i + 1) * 128], 1, keepdims=True)
        groups = jnp.where(lane == i, jnp.maximum(top, 0) // 128, groups)
    group_ref[...] = groups


def prepare_weights(
    cw_ref, qkvw_ref, ow_ref, g1_ref, g2_ref, w1_ref, cwt_ref, qkvt_ref, owt_ref, g1c_ref, g2c_ref, w1t_ref, pad
):
    for i in range(0, TAPS * C, 384):
        size = min(384, TAPS * C - i)
        cwt_ref[:, i : i + size] = cw_ref[i : i + size, :].astype(F32).T.astype(BF)
    wide = qkvw_ref[...].astype(F32).T
    pad[...] = jnp.zeros_like(pad)
    for j in range(3 * HEADS):
        pad[j * HP : j * HP + HD, :] = wide[j * HD : (j + 1) * HD, :]
    qkvt_ref[...] = pad[...].astype(BF)
    ow = ow_ref[...].astype(F32)
    for j in range(HEADS):
        pad[j * HP : j * HP + HD, :] = ow[j * HD : (j + 1) * HD, :]
    owt_ref[...] = pad[0 : HEADS * HP, :].T.astype(BF)
    g1c_ref[...] = jnp.broadcast_to(g1_ref[...], (128, C)).T
    g2c_ref[...] = jnp.broadcast_to(g2_ref[...], (128, C)).T
    w1t_ref[...] = w1_ref[...].astype(F32).T.astype(BF)


def halo_kernel(
    halo_ref, feats_ref, hp_ref, tap_ref, cw_ref, qkvw_ref, ow_ref, g1_ref, g2_ref, w1_ref,
    out_ref, fetch_ref, own_ref, away_ref, spot_ref, group_ref, blank_ref,
    cwt_ref, qkvt_ref, owt_ref, g1c_ref, g2c_ref, w1t_ref,
    onehot, send, zeros, pad, cw, qkvw, ow, w1, tap, cwt, send_sem, recv_sem, zero_sem, load_sem,
):
    barrier, count = greet()
    loads = [
        pltpu.make_async_copy(src, dst, load_sem.at[i])
        for i, (src, dst) in enumerate(
            ((cw_ref, cw), (qkvw_ref, qkvw), (ow_ref, ow), (w1_ref, w1), (tap_ref, tap))
        )
    ]
    for load in loads:
        load.start()
    zeros[...] = jnp.zeros_like(zeros)

    def start(k):
        inside = neighbour(k)[0]

        @pl.when(inside)
        def _():
            push(k, send.at[k], out_ref.at[7 - k], send_sem, recv_sem).start()

        @pl.when(jnp.logical_not(inside))
        def _():
            pltpu.make_async_copy(zeros, out_ref.at[k], zero_sem.at[k]).start()

    pl.semaphore_wait(barrier, count)

    def one(i, carry):
        pair = in_turn(i // 2)
        k = jnp.where(i % 2 == 0, pair, 7 - pair)
        select_columns(halo_ref[pl.ds(k, 1), :], onehot)
        send[k] = jnp.dot(feats_ref[...], onehot[...], preferred_element_type=F32).astype(BF)
        start(k)
        return carry

    lax.fori_loop(0, 8, one, 0)
    for load in loads:
        load.wait()
    prepare_weights(cw, qkvw, ow, g1_ref, g2_ref, w1, cwt, qkvt_ref, owt_ref, g1c_ref, g2c_ref, w1t_ref, pad)
    store = pltpu.make_async_copy(cwt, cwt_ref, load_sem.at[5])
    store.start()
    prepare_indices(hp_ref, tap, fetch_ref, own_ref, away_ref, spot_ref, group_ref, blank_ref)

    def finish(k):
        inside = neighbour(k)[0]

        @pl.when(inside)
        def _():
            push(k, send.at[k], out_ref.at[7 - k], send_sem, recv_sem).wait_send()
            push(7 - k, send.at[k], out_ref.at[k], send_sem, recv_sem).wait_recv()

        @pl.when(jnp.logical_not(inside))
        def _():
            pltpu.make_async_copy(zeros, out_ref.at[k], zero_sem.at[k]).wait()

    each(finish)
    store.wait()


def halo_exchange(halo, feats_t, hp, tap_t, cw, qkvw, ow, g1, g2, w1):
    sd = jax.ShapeDtypeStruct
    return pl.pallas_call(
        halo_kernel,
        name="halo_exchange",
        in_specs=[VM, VM, VM, ANY, ANY, ANY, ANY, VM, VM, ANY],
        out_specs=[ANY] + [VM] * 6 + [ANY] + [VM] * 5,
        out_shape=[
            sd((8, C, HB), BF),
            sd((32, 128), I32), sd((32, 128), I32), sd((32, 128), I32), sd((32, 128), I32),
            sd((TAPS, 128), I32), sd((SLOTS // 128, 128), I32),
            sd((C, TAPS * C), BF), sd((3 * HEADS * HP, C), BF), sd((C, HEADS * HP), BF),
            sd((C, 128), F32), sd((C, 128), F32), sd((4 * C, C), BF),
        ],
        scratch_shapes=[
            pltpu.VMEM((PTS, HB), BF),
            pltpu.VMEM((8, C, HB), BF),
            pltpu.VMEM((C, HB), BF),
            pltpu.VMEM((3 * HEADS * HP, C), F32),
            pltpu.VMEM((TAPS * C, C), BF),
            pltpu.VMEM((C, 3 * C), BF),
            pltpu.VMEM((C, C), BF),
            pltpu.VMEM((C, 4 * C), BF),
            pltpu.VMEM((TAPS, PTS), I32),
            pltpu.VMEM((C, TAPS * C), BF),
            pltpu.SemaphoreType.DMA((8,)),
            pltpu.SemaphoreType.DMA((8,)),
            pltpu.SemaphoreType.DMA((8,)),
            pltpu.SemaphoreType.DMA((6,)),
        ],
        compiler_params=params(collective_id=0, has_side_effects=True),
    )(halo, feats_t, hp, tap_t, cw, qkvw, ow, g1, g2, w1)


STEP = 2
PART = 128 * STEP
PARTS = PTS // PART
NOTES = -(-PART // (STEP * TAPS))


def conv_kernel(
    group_ref, fetch_ref, spot_ref, tap_ref, cwt_ref, feats_ref, halo_ref, blank_ref,
    out_ref, source_ref, lookup, even, odd, cwt, load_sem,
):
    weights = pltpu.make_async_copy(cwt_ref, cwt, load_sem.at[10])
    copies = [
        pltpu.make_async_copy(blank_ref, source_ref, load_sem.at[9]),
        pltpu.make_async_copy(feats_ref, lookup.at[:, 0:PTS], load_sem.at[8]),
    ]
    for k in range(8):
        at = PTS + k * HB
        copies.append(
            pltpu.make_async_copy(halo_ref.at[k], lookup.at[:, at : at + HB], load_sem.at[k])
        )
    for copy in copies:
        copy.start()
    weights.start()
    for r in range(PTS // 128):
        spot = spot_ref[r : r + 1, :] + 1
        number = lax.broadcasted_iota(I32, (ROWS - C, 128), 0)
        digits = jnp.where(number == 0, spot // 64, jnp.where(number == 1, spot % 64, 0))
        out_ref[C:ROWS, r * 128 : (r + 1) * 128] = digits.astype(F32).astype(BF)
    for copy in copies:
        copy.wait()
    weights.wait()

    def gather(i, gathered):
        for n in range(STEP):
            for t in range(TAPS):
                start = pl.multiple_of(group_ref[t, i * STEP + n] * 128, 128)
                source = lookup[:, pl.ds(start, 128)].astype(F32)
                lanes = pl.ds(pl.multiple_of(i * PART + n * 128, 128), 128)
                index = jnp.broadcast_to(tap_ref[t : t + 1, lanes], (C, 128))
                taken = jnp.take_along_axis(source, index & 127, axis=1)
                taken = jnp.where(index >= 0, taken, 0.0)
                gathered[t * C : (t + 1) * C, n * 128 : (n + 1) * 128] = taken.astype(BF)
                first = (n * TAPS + t) * NOTES
                points = [i * PART + u for u in range(first, min(first + NOTES, PART))]
                places = [fetch_ref[p] for p in points]
                for p, place in zip(points, places):
                    source_ref[place] = p

    def multiply(i, gathered):
        at = pl.ds(pl.multiple_of(i * PART, PART), PART)
        conv = jnp.dot(cwt[...], gathered[...], preferred_element_type=F32)
        out_ref[0:C, at] = (lookup[:, at].astype(F32) + conv).astype(BF)

    def two(j, carry):
        multiply(jnp.maximum(2 * j - 1, 0), odd)
        gather(2 * j, even)
        multiply(2 * j, even)
        gather(2 * j + 1, odd)
        return carry

    odd[...] = jnp.zeros_like(odd)
    lax.fori_loop(0, PARTS // 2, two, 0)
    multiply(PARTS - 1, odd)


def conv(groups, fetch, spot, tap_t, cwt, feats_t, halo, blank):
    sd = jax.ShapeDtypeStruct
    return pl.pallas_call(
        conv_kernel,
        name="conv",
        in_specs=[SM, SM, VM, VM, ANY, ANY, ANY, ANY],
        out_specs=[VM, SM],
        out_shape=[sd((ROWS, PTS), BF), sd((SLOTS,), I32)],
        scratch_shapes=[
            pltpu.VMEM((C, PTS + 8 * HB), BF),
            pltpu.VMEM((TAPS * C, PART), BF),
            pltpu.VMEM((TAPS * C, PART), BF),
            pltpu.VMEM((C, TAPS * C), BF),
            pltpu.SemaphoreType.DMA((11,)),
        ],
        compiler_params=params(),
    )(groups, fetch, spot, tap_t, cwt, feats_t, halo, blank)


BLOCK = 512


def deal_kernel(updated_ref, source_ref, out_ref, spots_ref, onehot_a, onehot_b, send, recv, send_sem, recv_sem):
    barrier, count = greet()

    def blank(k):
        @pl.when(jnp.logical_not(neighbour(k)[0]))
        def _():
            recv[k] = jnp.zeros((ROWS, CAP), BF)

    each(blank)

    def start(k):
        @pl.when(neighbour(k)[0])
        def _():
            push(k, send.at[k], recv.at[7 - k], send_sem, recv_sem).start()

    pl.semaphore_wait(barrier, count)
    first = onehot_a.at[:, 0:CAP]
    second = onehot_b.at[:, 0:CAP]

    def pair(i, carry):
        k = in_turn(i)
        base = PTS // 128
        select_columns(index_row(source_ref, base + k * (CAP // 128), CAP // 128), first)
        select_columns(index_row(source_ref, base + (7 - k) * (CAP // 128), CAP // 128), second)

        send[k] = jnp.dot(updated_ref[...], first[...], preferred_element_type=F32).astype(BF)
        send[7 - k] = jnp.dot(updated_ref[...], second[...], preferred_element_type=F32).astype(BF)
        start(k)
        start(7 - k)
        return carry

    lax.fori_loop(0, 4, pair, 0)

    def stay(m, carry):
        for n, onehot in ((2 * m, onehot_a), (2 * m + 1, onehot_b)):
            select_columns(index_row(source_ref, n * (BLOCK // 128), BLOCK // 128), onehot)
        for n, onehot in ((2 * m, onehot_a), (2 * m + 1, onehot_b)):
            taken = jnp.dot(updated_ref[0:C, :], onehot[...], preferred_element_type=F32)
            out_ref[:, pl.ds(pl.multiple_of(n * BLOCK, BLOCK), BLOCK)] = taken.astype(BF)
        return carry

    lax.fori_loop(0, PTS // BLOCK // 2, stay, 0)

    def finish(k):
        @pl.when(neighbour(k)[0])
        def _():
            push(k, send.at[k], recv.at[7 - k], send_sem, recv_sem).wait_send()
            push(7 - k, send.at[k], recv.at[k], send_sem, recv_sem).wait_recv()

    each(finish)

    for k in range(8):
        digits = recv[k, C:ROWS, :].astype(F32)
        spots_ref[k : k + 1, :] = (digits[0:1, :] * 64.0 + digits[1:2, :] - 1.0).astype(I32)

    def arrive(n, carry):
        total = jnp.zeros((C, BLOCK), F32)
        at = pl.multiple_of(n * BLOCK, BLOCK)
        place = lax.broadcasted_iota(I32, (BLOCK, CAP), 0) + at
        for k in range(8):
            chosen = jnp.where(place == spots_ref[k : k + 1, :], 1.0, 0.0).astype(BF)
            total = total + lax.dot_general(
                recv[k, 0:C, :], chosen, (((1,), (1,)), ((), ())), preferred_element_type=F32
            )
        here = out_ref[:, pl.ds(at, BLOCK)].astype(F32) + total
        out_ref[:, pl.ds(at, BLOCK)] = here.astype(BF)
        return carry

    lax.fori_loop(0, PTS // BLOCK, arrive, 0)


def deal(updated, source):
    sd = jax.ShapeDtypeStruct
    return pl.pallas_call(
        deal_kernel,
        name="deal",
        in_specs=[VM, VM],
        out_specs=[VM, VM],
        out_shape=[sd((C, PTS), BF), sd((8, CAP), I32)],
        scratch_shapes=[
            pltpu.VMEM((PTS, BLOCK), BF),
            pltpu.VMEM((PTS, BLOCK), BF),
            pltpu.VMEM((8, ROWS, CAP), BF),
            pltpu.VMEM((8, ROWS, CAP), BF),
            pltpu.SemaphoreType.DMA((8,)),
            pltpu.SemaphoreType.DMA((8,)),
        ],
        compiler_params=params(collective_id=1, has_side_effects=True),
    )(updated, source)


def norm_columns(values, gain):
    average = jnp.sum(values, 0, keepdims=True) * (1.0 / C)
    centred = values - average
    variance = jnp.sum(centred * centred, 0, keepdims=True) * (1.0 / C)
    return (centred * lax.rsqrt(variance + 1e-05) * gain).astype(BF)


def window_kernel(
    in_ref, g1_ref, qkvt_ref, owt_ref, g2_ref, w1t_ref, w2t_ref, out_ref, packed, attended
):
    def window(w, carry):
        base = pl.multiple_of(w * WIN, WIN)
        x = in_ref[:, pl.ds(base, WIN)].astype(F32)
        normed = norm_columns(x, g1_ref[:, 0:1])
        wide = HEADS * HP
        queries = jnp.dot(qkvt_ref[0:wide, :], normed, preferred_element_type=F32) * SCALE
        packed[0:wide, :] = queries.astype(BF)
        packed[wide : 3 * wide, :] = jnp.dot(
            qkvt_ref[wide : 3 * wide, :], normed, preferred_element_type=F32
        ).astype(BF)
        largest_q = jnp.zeros((1, WIN), F32)
        largest_k = jnp.zeros((1, WIN), F32)
        for h in range(HEADS):
            q = packed[h * HP : (h + 1) * HP, :].astype(F32)
            key = packed[wide + h * HP : wide + (h + 1) * HP, :].astype(F32)
            largest_q = jnp.maximum(largest_q, jnp.sum(q * q, 0, keepdims=True))
            largest_k = jnp.maximum(largest_k, jnp.sum(key * key, 0, keepdims=True))
        safe = jnp.max(largest_q) * jnp.max(largest_k) <= SAFE * SAFE

        def heads(shifted):
            def head(h, inner):
                off = pl.multiple_of(h * HP, HP)
                q = packed[pl.ds(off, HP), :]
                key = packed[pl.ds(wide + off, HP), :]
                value = packed[pl.ds(2 * wide + off, HP), :]
                number = lax.broadcasted_iota(I32, (HP, WIN), 0)
                value = jnp.where(number == HD, jnp.ones_like(value), value)
                scores = lax.dot_general(
                    key, q, (((0,), (0,)), ((), ())), preferred_element_type=F32
                )
                if shifted:
                    scores = scores - jnp.max(scores, 0, keepdims=True)
                probs = jnp.exp2(scores).astype(BF)
                mixed = jnp.dot(value, probs, preferred_element_type=F32)
                attended[pl.ds(off, HP), :] = (mixed / mixed[HD : HD + 1, :]).astype(BF)
                return inner

            lax.fori_loop(0, HEADS, head, 0, unroll=1 if shifted else 4)

        @pl.when(safe)
        def _():
            heads(False)

        @pl.when(jnp.logical_not(safe))
        def _():
            heads(True)

        residual = x + jnp.dot(owt_ref[...], attended[...], preferred_element_type=F32)
        residual = residual.astype(BF).astype(F32)
        normed_two = norm_columns(residual, g2_ref[:, 0:1])
        hidden = jnp.dot(w1t_ref[...], normed_two, preferred_element_type=F32)
        hidden = 0.5 * hidden * (1.0 + lax.erf(hidden * (2.0**-0.5)))
        processed = residual + jnp.dot(w2t_ref[...], hidden.astype(BF), preferred_element_type=F32)
        out_ref[:, pl.ds(base, WIN)] = processed.astype(BF)
        return carry

    lax.fori_loop(0, PTS // WIN, window, 0)


def windows(ordered, g1, qkvt, owt, g2, w1t, w2t):
    return pl.pallas_call(
        window_kernel,
        name="windows",
        in_specs=[VM] * 7,
        out_specs=VM,
        out_shape=jax.ShapeDtypeStruct((C, PTS), BF),
        scratch_shapes=[
            pltpu.VMEM((3 * HEADS * HP, WIN), BF),
            pltpu.VMEM((HEADS * HP, WIN), BF),
        ],
        compiler_params=params(),
    )(ordered, g1, qkvt, owt, g2, w1t, w2t)


def back_kernel(done_ref, spots_ref, own_ref, out_ref, recv, onehot_a, onehot_b, send, send_sem, recv_sem):
    barrier, count = greet()

    def landing(k):
        return recv.at[:, pl.ds(pl.multiple_of(k * CAP, CAP), CAP)]

    def blank(k):
        @pl.when(jnp.logical_not(neighbour(k)[0]))
        def _():
            recv[:, pl.ds(pl.multiple_of(k * CAP, CAP), CAP)] = jnp.zeros((C, CAP), BF)

    each(blank)

    def start(k):
        @pl.when(neighbour(k)[0])
        def _():
            push(k, send.at[k], landing(7 - k), send_sem, recv_sem).start()

    pl.semaphore_wait(barrier, count)
    first = onehot_a.at[:, 0:CAP]
    second = onehot_b.at[:, 0:CAP]

    def pair(i, carry):
        k = in_turn(i)
        select_columns(spots_ref[pl.ds(k, 1), :], first)
        select_columns(spots_ref[pl.ds(7 - k, 1), :], second)

        send[k] = jnp.dot(done_ref[...], first[...], preferred_element_type=F32).astype(BF)
        send[7 - k] = jnp.dot(done_ref[...], second[...], preferred_element_type=F32).astype(BF)
        start(k)
        start(7 - k)
        return carry

    lax.fori_loop(0, 4, pair, 0)

    def stay(m, carry):
        for n, onehot in ((2 * m, onehot_a), (2 * m + 1, onehot_b)):
            select_columns(index_row(own_ref, n * (BLOCK // 128), BLOCK // 128), onehot)
        for n, onehot in ((2 * m, onehot_a), (2 * m + 1, onehot_b)):
            taken = jnp.dot(done_ref[...], onehot[...], preferred_element_type=F32)
            out_ref[:, pl.ds(pl.multiple_of(n * BLOCK, BLOCK), BLOCK)] = taken.astype(BF)
        return carry

    lax.fori_loop(0, PTS // BLOCK // 2, stay, 0)

    def finish(k):
        @pl.when(neighbour(k)[0])
        def _():
            push(k, send.at[k], landing(7 - k), send_sem, recv_sem).wait_send()
            push(7 - k, send.at[k], landing(k), send_sem, recv_sem).wait_recv()

    each(finish)


def back(done, spots, own):
    sd = jax.ShapeDtypeStruct
    return pl.pallas_call(
        back_kernel,
        name="back",
        in_specs=[VM] * 3,
        out_specs=[VM, VM],
        out_shape=[sd((C, PTS), BF), sd((C, 8 * CAP), BF)],
        scratch_shapes=[
            pltpu.VMEM((PTS, BLOCK), BF),
            pltpu.VMEM((PTS, BLOCK), BF),
            pltpu.VMEM((8, C, CAP), BF),
            pltpu.SemaphoreType.DMA((8,)),
            pltpu.SemaphoreType.DMA((8,)),
        ],
        compiler_params=params(collective_id=2, has_side_effects=True),
    )(done, spots, own)


WIDE = 1024


def collect_kernel(kept_ref, returned_ref, away_ref, out_ref, onehot_a, onehot_b):
    i = pl.program_id(0)
    halves = ((0, onehot_a), (BLOCK, onehot_b))
    for at, onehot in halves:
        first = i * (WIDE // 128) + at // 128
        select_columns(index_row(away_ref, first, BLOCK // 128), onehot)
    for at, onehot in halves:
        taken = jnp.dot(returned_ref[...], onehot[...], preferred_element_type=F32)
        kept = kept_ref[:, at : at + BLOCK].astype(F32)
        out_ref[:, at : at + BLOCK] = (kept + taken).astype(BF)


def collect(kept, returned, away):
    return pl.pallas_call(
        collect_kernel,
        name="collect",
        grid=(PTS // WIDE,),
        in_specs=[
            pl.BlockSpec((C, WIDE), lambda i: (0, i)),
            pl.BlockSpec((C, 8 * CAP), lambda i: (0, 0)),
            pl.BlockSpec((32, 128), lambda i: (0, 0)),
        ],
        out_specs=pl.BlockSpec((C, WIDE), lambda i: (0, i)),
        out_shape=jax.ShapeDtypeStruct((C, PTS), BF),
        scratch_shapes=[pltpu.VMEM((8 * CAP, BLOCK), BF), pltpu.VMEM((8 * CAP, BLOCK), BF)],
        compiler_params=params(dimension_semantics=("arbitrary",)),
    )(kept, returned, away)


def on_device(
    feats, conv_weight, tap_index, halo_rows, hilbert_pos,
    ln1_gain, qkv_weight, out_weight, ln2_gain, mlp_in, mlp_out,
):
    feats_t = feats.T
    tap_t = tap_index.T
    halo, fetch, own, away, spot, groups, blank, cwt, qkvt, owt, g1, g2, w1t = halo_exchange(
        halo_rows[0], feats_t, hilbert_pos.reshape(32, 128), tap_t,
        conv_weight.reshape(TAPS * C, C), qkv_weight, out_weight,
        ln1_gain.reshape(1, C), ln2_gain.reshape(1, C), mlp_in,
    )
    updated, source = conv(
        groups, fetch.reshape(PTS), spot, tap_t, cwt, feats_t, halo,
        blank.reshape(SLOTS),
    )
    ordered, spots = deal(updated, source.reshape(SLOTS // 128, 128))
    done = windows(ordered, g1, qkvt, owt, g2, w1t, mlp_out.T)
    kept, returned = back(done, spots, own)
    return collect(kept, returned, away).T


def solution(mesh):
    rows = P(("gx", "gy"), None)
    placed = (rows, P(), rows, P(("gx", "gy"), None, None), P(("gx", "gy"))) + (P(),) * 6
    return jax.shard_map(
        on_device, mesh=mesh, in_specs=placed, out_specs=rows, check_vma=False
    )
```

```python
import functools
import math

import jax
import jax.numpy as jnp
from jax import lax
from jax.experimental import pallas as pl
from jax.experimental.pallas import tpu as pltpu
from jax.sharding import PartitionSpec as P

BF = jnp.bfloat16
F32 = jnp.float32
I32 = jnp.int32
MESH = pl.DeviceIdType.MESH

C = 192
HEADS = 8
HD = 24
HP = 32
WIN = 1024
TAPS = 27
PTS = 4096
HB = 512
CAP = PTS // 16
GROUP = 128
ROWS = C + 16
VMEM_LIMIT = 60 * 1024 * 1024
SCALE = 1.0 / math.sqrt(HD) * math.log2(math.e)
SAFE = 80.0


def params(**kw):
    return pltpu.CompilerParams(vmem_limit_bytes=VMEM_LIMIT, **kw)


VM = pl.BlockSpec(memory_space=pltpu.VMEM)
SM = pl.BlockSpec(memory_space=pltpu.SMEM)
ANY = pl.BlockSpec(memory_space=pl.ANY)


def neighbour(k):
    j = k + k // 4
    x = lax.axis_index("gx") + j // 3 - 1
    y = lax.axis_index("gy") + j % 3 - 1
    inside = (x >= 0) & (x < lax.axis_size("gx")) & (y >= 0) & (y < lax.axis_size("gy"))
    return inside, x, y


def in_turn(i):
    return i + jnp.minimum(i, 1) - 3 * (i // 3)


def greet():
    barrier = pltpu.get_barrier_semaphore()
    count = jnp.int32(0)
    for k in range(8):
        inside, x, y = neighbour(k)
        count = count + inside.astype(I32)

        @pl.when(inside)
        def _():
            pl.semaphore_signal(barrier, inc=1, device_id=(x, y), device_id_type=MESH)

    return barrier, count


def push(k, src, dst, send_sem, recv_sem):
    _, x, y = neighbour(k)
    return pltpu.make_async_remote_copy(
        src_ref=src, dst_ref=dst, send_sem=send_sem.at[k], recv_sem=recv_sem.at[7 - k],
        device_id=(x, y), device_id_type=MESH,
    )


def each(body):
    def step(k, carry):
        body(k)
        return carry

    lax.fori_loop(0, 8, step, 0)


def index_row(ref, first, count):
    return jnp.concatenate([ref[pl.ds(first + u, 1), :] for u in range(count)], 1)


def select_columns(index, onehot):
    depth, width = onehot.shape
    for s in range(0, depth, 256):
        place = lax.broadcasted_iota(I32, (256, width), 0) + s
        onehot[s : s + 256, :] = jnp.where(place == index, 1.0, 0.0).astype(BF)


def spread_index(row):
    return jnp.broadcast_to(row, (128, row.shape[1])).T


def place_rows(index, base, onehot):
    depth, width = onehot.shape
    for s in range(0, depth, 256):
        here = index[s : s + 256, :] - base
        hits = [
            jnp.where(lax.broadcasted_iota(I32, (256, 128), 1) + d == here, 1.0, 0.0)
            for d in range(0, width, 128)
        ]
        onehot[s : s + 256, :] = jnp.concatenate(hits, 1).astype(BF)


def prepare_indices(hp_ref, tap_ref, fetch_ref, own_ref, away_ref, spot_ref, group_ref):
    ix = lax.axis_index("gx")
    iy = lax.axis_index("gy")
    ny = lax.axis_size("gy")
    hp = hp_ref[...]
    target = hp // PTS
    local = hp - target * PTS
    step_x = target // ny - ix
    step_y = target % ny - iy
    code = 3 * (step_x + 1) + (step_y + 1)
    r128 = lax.broadcasted_iota(I32, (128, 128), 0)
    c128 = lax.broadcasted_iota(I32, (128, 128), 1)
    tri = (r128 < c128).astype(F32).astype(BF)
    r32 = lax.broadcasted_iota(I32, (32, 32), 0)
    c32 = lax.broadcasted_iota(I32, (32, 32), 1)
    low = (c32 < r32).astype(F32).astype(BF)
    before = jnp.zeros((32, 128), F32)
    for c in range(9):
        if c == 4:
            continue
        m = (code == c).astype(F32)
        mb = m.astype(BF)
        within = jnp.dot(mb, tri, preferred_element_type=F32)
        above = jnp.sum(jnp.dot(low, mb, preferred_element_type=F32), 1, keepdims=True)
        before = before + m * (within + above)
    away = (code - (code > 4).astype(I32)) * CAP + before.astype(I32)
    own = code == 4
    fetch_ref[...] = jnp.where(own, local, PTS + away)
    own_ref[...] = jnp.where(own, local, -1)
    away_ref[...] = jnp.where(own, -1, away)
    spot_ref[...] = local
    lane = lax.broadcasted_iota(I32, (TAPS, 128), 1)
    groups = jnp.zeros((TAPS, 128), I32)
    for i in range(PTS // 128):
        top = jnp.max(tap_ref[:, i * 128 : (i + 1) * 128], 1, keepdims=True)
        groups = jnp.where(lane == i, jnp.maximum(top, 0) // 128, groups)
    group_ref[...] = groups


def prepare_weights(
    cw_ref, qkvw_ref, ow_ref, g1_ref, g2_ref, w1_ref, cwt_ref, qkvt_ref, owt_ref, g1c_ref, g2c_ref, w1t_ref, pad
):
    for i in range(0, TAPS * C, 384):
        size = min(384, TAPS * C - i)
        cwt_ref[:, i : i + size] = cw_ref[i : i + size, :].astype(F32).T.astype(BF)
    wide = qkvw_ref[...].astype(F32).T
    pad[...] = jnp.zeros_like(pad)
    for j in range(3 * HEADS):
        pad[j * HP : j * HP + HD, :] = wide[j * HD : (j + 1) * HD, :]
    qkvt_ref[...] = pad[...].astype(BF)
    ow = ow_ref[...].astype(F32)
    for j in range(HEADS):
        pad[j * HP : j * HP + HD, :] = ow[j * HD : (j + 1) * HD, :]
    owt_ref[...] = pad[0 : HEADS * HP, :].T.astype(BF)
    g1c_ref[...] = jnp.broadcast_to(g1_ref[...], (128, C)).T
    g2c_ref[...] = jnp.broadcast_to(g2_ref[...], (128, C)).T
    w1t_ref[...] = w1_ref[...].astype(F32).T.astype(BF)


def halo_kernel(
    halo_ref, feats_ref, hp_ref, tap_ref, cw_ref, qkvw_ref, ow_ref, g1_ref, g2_ref, w1_ref,
    out_ref, fetch_ref, own_ref, away_ref, spot_ref, group_ref,
    cwt_ref, qkvt_ref, owt_ref, g1c_ref, g2c_ref, w1t_ref,
    onehot, send, zeros, pad, cw, qkvw, ow, w1, tap, cwt, send_sem, recv_sem, zero_sem, load_sem,
):
    barrier, count = greet()
    loads = [
        pltpu.make_async_copy(src, dst, load_sem.at[i])
        for i, (src, dst) in enumerate(
            ((cw_ref, cw), (qkvw_ref, qkvw), (ow_ref, ow), (w1_ref, w1), (tap_ref, tap))
        )
    ]
    for load in loads:
        load.start()
    zeros[...] = jnp.zeros_like(zeros)

    def start(k):
        inside = neighbour(k)[0]

        @pl.when(inside)
        def _():
            push(k, send.at[k], out_ref.at[7 - k], send_sem, recv_sem).start()

        @pl.when(jnp.logical_not(inside))
        def _():
            pltpu.make_async_copy(zeros, out_ref.at[k], zero_sem.at[k]).start()

    pl.semaphore_wait(barrier, count)

    def one(i, carry):
        pair = in_turn(i // 2)
        k = jnp.where(i % 2 == 0, pair, 7 - pair)
        select_columns(halo_ref[pl.ds(k, 1), :], onehot)
        send[k] = jnp.dot(feats_ref[...], onehot[...], preferred_element_type=F32).astype(BF)
        start(k)
        return carry

    lax.fori_loop(0, 8, one, 0)
    for load in loads:
        load.wait()
    prepare_weights(cw, qkvw, ow, g1_ref, g2_ref, w1, cwt, qkvt_ref, owt_ref, g1c_ref, g2c_ref, w1t_ref, pad)
    store = pltpu.make_async_copy(cwt, cwt_ref, load_sem.at[5])
    store.start()
    prepare_indices(hp_ref, tap, fetch_ref, own_ref, away_ref, spot_ref, group_ref)

    def finish(k):
        inside = neighbour(k)[0]

        @pl.when(inside)
        def _():
            push(k, send.at[k], out_ref.at[7 - k], send_sem, recv_sem).wait_send()
            push(7 - k, send.at[k], out_ref.at[k], send_sem, recv_sem).wait_recv()

        @pl.when(jnp.logical_not(inside))
        def _():
            pltpu.make_async_copy(zeros, out_ref.at[k], zero_sem.at[k]).wait()

    each(finish)
    store.wait()


def halo_exchange(halo, feats_t, hp, tap_t, cw, qkvw, ow, g1, g2, w1):
    sd = jax.ShapeDtypeStruct
    return pl.pallas_call(
        halo_kernel,
        name="halo_exchange",
        in_specs=[VM, VM, VM, ANY, ANY, ANY, ANY, VM, VM, ANY],
        out_specs=[ANY] + [VM] * 5 + [ANY] + [VM] * 5,
        out_shape=[
            sd((8, C, HB), BF),
            sd((32, 128), I32), sd((32, 128), I32), sd((32, 128), I32), sd((32, 128), I32),
            sd((TAPS, 128), I32),
            sd((C, TAPS * C), BF), sd((3 * HEADS * HP, C), BF), sd((C, HEADS * HP), BF),
            sd((C, 128), F32), sd((C, 128), F32), sd((4 * C, C), BF),
        ],
        scratch_shapes=[
            pltpu.VMEM((PTS, HB), BF),
            pltpu.VMEM((8, C, HB), BF),
            pltpu.VMEM((C, HB), BF),
            pltpu.VMEM((3 * HEADS * HP, C), F32),
            pltpu.VMEM((TAPS * C, C), BF),
            pltpu.VMEM((C, 3 * C), BF),
            pltpu.VMEM((C, C), BF),
            pltpu.VMEM((C, 4 * C), BF),
            pltpu.VMEM((TAPS, PTS), I32),
            pltpu.VMEM((C, TAPS * C), BF),
            pltpu.SemaphoreType.DMA((8,)),
            pltpu.SemaphoreType.DMA((8,)),
            pltpu.SemaphoreType.DMA((8,)),
            pltpu.SemaphoreType.DMA((6,)),
        ],
        compiler_params=params(collective_id=0, has_side_effects=True),
    )(halo, feats_t, hp, tap_t, cw, qkvw, ow, g1, g2, w1)


STEP = 2
PART = 128 * STEP
PARTS = PTS // PART


def conv_kernel(
    group_ref, spot_ref, tap_ref, cwt_ref, feats_ref, halo_ref, out_ref, lookup, even, odd, cwt, load_sem,
):
    weights = pltpu.make_async_copy(cwt_ref, cwt, load_sem.at[9])
    copies = [
        pltpu.make_async_copy(feats_ref, lookup.at[:, 0:PTS], load_sem.at[8]),
    ]
    for k in range(8):
        at = PTS + k * HB
        copies.append(
            pltpu.make_async_copy(halo_ref.at[k], lookup.at[:, at : at + HB], load_sem.at[k])
        )
    for copy in copies:
        copy.start()
    weights.start()
    for r in range(PTS // 128):
        spot = spot_ref[r : r + 1, :] + 1
        number = lax.broadcasted_iota(I32, (ROWS - C, 128), 0)
        digits = jnp.where(number == 0, spot // 64, jnp.where(number == 1, spot % 64, 0))
        out_ref[C:ROWS, r * 128 : (r + 1) * 128] = digits.astype(F32).astype(BF)
    for copy in copies:
        copy.wait()
    weights.wait()

    def gather(i, gathered):
        for n in range(STEP):
            for t in range(TAPS):
                start = pl.multiple_of(group_ref[t, i * STEP + n] * 128, 128)
                source = lookup[:, pl.ds(start, 128)].astype(F32)
                lanes = pl.ds(pl.multiple_of(i * PART + n * 128, 128), 128)
                index = jnp.broadcast_to(tap_ref[t : t + 1, lanes], (C, 128))
                taken = jnp.take_along_axis(source, index & 127, axis=1)
                taken = jnp.where(index >= 0, taken, 0.0)
                gathered[t * C : (t + 1) * C, n * 128 : (n + 1) * 128] = taken.astype(BF)

    def multiply(i, gathered):
        at = pl.ds(pl.multiple_of(i * PART, PART), PART)
        conv = jnp.dot(cwt[...], gathered[...], preferred_element_type=F32)
        out_ref[0:C, at] = (lookup[:, at].astype(F32) + conv).astype(BF)

    def two(j, carry):
        multiply(jnp.maximum(2 * j - 1, 0), odd)
        gather(2 * j, even)
        multiply(2 * j, even)
        gather(2 * j + 1, odd)
        return carry

    odd[...] = jnp.zeros_like(odd)
    lax.fori_loop(0, PARTS // 2, two, 0)
    multiply(PARTS - 1, odd)


def conv(groups, spot, tap_t, cwt, feats_t, halo):
    return pl.pallas_call(
        conv_kernel,
        name="conv",
        in_specs=[SM, VM, VM, ANY, ANY, ANY],
        out_specs=VM,
        out_shape=jax.ShapeDtypeStruct((ROWS, PTS), BF),
        scratch_shapes=[
            pltpu.VMEM((C, PTS + 8 * HB), BF),
            pltpu.VMEM((TAPS * C, PART), BF),
            pltpu.VMEM((TAPS * C, PART), BF),
            pltpu.VMEM((C, TAPS * C), BF),
            pltpu.SemaphoreType.DMA((10,)),
        ],
        compiler_params=params(),
    )(groups, spot, tap_t, cwt, feats_t, halo)


BLOCK = 512


def deal_kernel(
    updated_ref, fetch_ref, out_ref, spots_ref, index, onehot_a, onehot_b, send, recv, send_sem, recv_sem
):
    barrier, count = greet()

    def landing(k):
        return recv.at[:, pl.ds(pl.multiple_of(k * CAP, CAP), CAP)]

    def blank(k):
        @pl.when(jnp.logical_not(neighbour(k)[0]))
        def _():
            recv[:, pl.ds(pl.multiple_of(k * CAP, CAP), CAP)] = jnp.zeros((ROWS, CAP), BF)

    each(blank)

    def start(k):
        @pl.when(neighbour(k)[0])
        def _():
            push(k, send.at[k], landing(7 - k), send_sem, recv_sem).start()

    for r in range(PTS // 128):
        index[r * 128 : (r + 1) * 128, :] = spread_index(fetch_ref[r : r + 1, :])
    pl.semaphore_wait(barrier, count)
    first = onehot_a.at[:, 0:CAP]
    second = onehot_b.at[:, 0:CAP]

    def pair(i, carry):
        k = in_turn(i)
        place_rows(index, PTS + k * CAP, first)
        place_rows(index, PTS + (7 - k) * CAP, second)

        send[k] = jnp.dot(updated_ref[...], first[...], preferred_element_type=F32).astype(BF)
        send[7 - k] = jnp.dot(updated_ref[...], second[...], preferred_element_type=F32).astype(BF)
        start(k)
        start(7 - k)
        return carry

    lax.fori_loop(0, 4, pair, 0)

    def stay(m, carry):
        for n, onehot in ((2 * m, onehot_a), (2 * m + 1, onehot_b)):
            place_rows(index, n * BLOCK, onehot)
        for n, onehot in ((2 * m, onehot_a), (2 * m + 1, onehot_b)):
            taken = jnp.dot(updated_ref[0:C, :], onehot[...], preferred_element_type=F32)
            out_ref[:, pl.ds(pl.multiple_of(n * BLOCK, BLOCK), BLOCK)] = taken.astype(BF)
        return carry

    lax.fori_loop(0, PTS // BLOCK // 2, stay, 0)

    def finish(k):
        @pl.when(neighbour(k)[0])
        def _():
            push(k, send.at[k], landing(7 - k), send_sem, recv_sem).wait_send()
            push(7 - k, send.at[k], landing(k), send_sem, recv_sem).wait_recv()

    each(finish)

    depth = 8 * CAP
    for k in range(8):
        digits = recv[C:ROWS, k * CAP : (k + 1) * CAP].astype(F32)
        spot = (digits[0:1, :] * 64.0 + digits[1:2, :] - 1.0).astype(I32)
        spots_ref[k : k + 1, :] = spot
        for c in range(0, CAP, 128):
            at = k * CAP + c
            index[at : at + 128, :] = spread_index(spot[:, c : c + 128])

    def arrive(m, carry):
        blocks = ((2 * m, onehot_a), (2 * m + 1, onehot_b))
        for n, onehot in blocks:
            place_rows(index, n * BLOCK, onehot.at[0:depth, :])
        for n, onehot in blocks:
            at = pl.ds(pl.multiple_of(n * BLOCK, BLOCK), BLOCK)
            taken = jnp.dot(recv[0:C, :], onehot[0:depth, :], preferred_element_type=F32)
            out_ref[:, at] = (out_ref[:, at].astype(F32) + taken).astype(BF)
        return carry

    lax.fori_loop(0, PTS // BLOCK // 2, arrive, 0)


def deal(updated, fetch):
    sd = jax.ShapeDtypeStruct
    return pl.pallas_call(
        deal_kernel,
        name="deal",
        in_specs=[VM, VM],
        out_specs=[VM, VM],
        out_shape=[sd((C, PTS), BF), sd((8, CAP), I32)],
        scratch_shapes=[
            pltpu.VMEM((PTS, 128), I32),
            pltpu.VMEM((PTS, BLOCK), BF),
            pltpu.VMEM((PTS, BLOCK), BF),
            pltpu.VMEM((8, ROWS, CAP), BF),
            pltpu.VMEM((ROWS, 8 * CAP), BF),
            pltpu.SemaphoreType.DMA((8,)),
            pltpu.SemaphoreType.DMA((8,)),
        ],
        compiler_params=params(collective_id=1, has_side_effects=True),
    )(updated, fetch)


def norm_columns(values, gain):
    average = jnp.sum(values, 0, keepdims=True) * (1.0 / C)
    centred = values - average
    variance = jnp.sum(centred * centred, 0, keepdims=True) * (1.0 / C)
    return (centred * lax.rsqrt(variance + 1e-05) * gain).astype(BF)


def window_kernel(
    in_ref, g1_ref, qkvt_ref, owt_ref, g2_ref, w1t_ref, w2t_ref, out_ref, packed, attended
):
    x = in_ref[...].astype(F32)
    normed = norm_columns(x, g1_ref[:, 0:1])
    wide = HEADS * HP
    queries = jnp.dot(qkvt_ref[0:wide, :], normed, preferred_element_type=F32) * SCALE
    packed[0:wide, :] = queries.astype(BF)
    packed[wide : 3 * wide, :] = jnp.dot(
        qkvt_ref[wide : 3 * wide, :], normed, preferred_element_type=F32
    ).astype(BF)
    largest_q = jnp.zeros((1, WIN), F32)
    largest_k = jnp.zeros((1, WIN), F32)
    for h in range(HEADS):
        q = packed[h * HP : (h + 1) * HP, :].astype(F32)
        key = packed[wide + h * HP : wide + (h + 1) * HP, :].astype(F32)
        largest_q = jnp.maximum(largest_q, jnp.sum(q * q, 0, keepdims=True))
        largest_k = jnp.maximum(largest_k, jnp.sum(key * key, 0, keepdims=True))
    safe = jnp.max(largest_q) * jnp.max(largest_k) <= SAFE * SAFE

    def heads(shifted):
        def head(h, inner):
            off = pl.multiple_of(h * HP, HP)
            q = packed[pl.ds(off, HP), :]
            key = packed[pl.ds(wide + off, HP), :]
            value = packed[pl.ds(2 * wide + off, HP), :]
            number = lax.broadcasted_iota(I32, (HP, WIN), 0)
            value = jnp.where(number == HD, jnp.ones_like(value), value)
            scores = lax.dot_general(
                key, q, (((0,), (0,)), ((), ())), preferred_element_type=F32
            )
            if shifted:
                scores = scores - jnp.max(scores, 0, keepdims=True)
            probs = jnp.exp2(scores).astype(BF)
            mixed = jnp.dot(value, probs, preferred_element_type=F32)
            attended[pl.ds(off, HP), :] = (mixed / mixed[HD : HD + 1, :]).astype(BF)
            return inner

        lax.fori_loop(0, HEADS, head, 0, unroll=1 if shifted else 8)

    @pl.when(safe)
    def _():
        heads(False)

    @pl.when(jnp.logical_not(safe))
    def _():
        heads(True)

    residual = x + jnp.dot(owt_ref[...], attended[...], preferred_element_type=F32)
    residual = residual.astype(BF).astype(F32)
    normed_two = norm_columns(residual, g2_ref[:, 0:1])
    hidden = jnp.dot(w1t_ref[...], normed_two, preferred_element_type=F32)
    hidden = 0.5 * hidden * (1.0 + lax.erf(hidden * (2.0**-0.5)))
    processed = residual + jnp.dot(w2t_ref[...], hidden.astype(BF), preferred_element_type=F32)
    out_ref[...] = processed.astype(BF)


def windows(ordered, g1, qkvt, owt, g2, w1t, w2t):
    return pl.pallas_call(
        window_kernel,
        name="windows",
        grid=(PTS // WIN,),
        in_specs=[pl.BlockSpec((C, WIN), lambda i: (0, i)), VM, VM, VM, VM, VM, VM],
        out_specs=pl.BlockSpec((C, WIN), lambda i: (0, i)),
        out_shape=jax.ShapeDtypeStruct((C, PTS), BF),
        scratch_shapes=[
            pltpu.VMEM((3 * HEADS * HP, WIN), BF),
            pltpu.VMEM((HEADS * HP, WIN), BF),
        ],
        compiler_params=params(dimension_semantics=("arbitrary",)),
    )(ordered, g1, qkvt, owt, g2, w1t, w2t)


def back_kernel(done_ref, spots_ref, own_ref, out_ref, recv, onehot_a, onehot_b, send, send_sem, recv_sem):
    barrier, count = greet()

    def landing(k):
        return recv.at[:, pl.ds(pl.multiple_of(k * CAP, CAP), CAP)]

    def blank(k):
        @pl.when(jnp.logical_not(neighbour(k)[0]))
        def _():
            recv[:, pl.ds(pl.multiple_of(k * CAP, CAP), CAP)] = jnp.zeros((C, CAP), BF)

    each(blank)

    def start(k):
        @pl.when(neighbour(k)[0])
        def _():
            push(k, send.at[k], landing(7 - k), send_sem, recv_sem).start()

    pl.semaphore_wait(barrier, count)
    first = onehot_a.at[:, 0:CAP]
    second = onehot_b.at[:, 0:CAP]

    def pair(i, carry):
        k = in_turn(i)
        select_columns(spots_ref[pl.ds(k, 1), :], first)
        select_columns(spots_ref[pl.ds(7 - k, 1), :], second)

        send[k] = jnp.dot(done_ref[...], first[...], preferred_element_type=F32).astype(BF)
        send[7 - k] = jnp.dot(done_ref[...], second[...], preferred_element_type=F32).astype(BF)
        start(k)
        start(7 - k)
        return carry

    lax.fori_loop(0, 4, pair, 0)

    def stay(m, carry):
        for n, onehot in ((2 * m, onehot_a), (2 * m + 1, onehot_b)):
            select_columns(index_row(own_ref, n * (BLOCK // 128), BLOCK // 128), onehot)
        for n, onehot in ((2 * m, onehot_a), (2 * m + 1, onehot_b)):
            taken = jnp.dot(done_ref[...], onehot[...], preferred_element_type=F32)
            out_ref[:, pl.ds(pl.multiple_of(n * BLOCK, BLOCK), BLOCK)] = taken.astype(BF)
        return carry

    lax.fori_loop(0, PTS // BLOCK // 2, stay, 0)

    def finish(k):
        @pl.when(neighbour(k)[0])
        def _():
            push(k, send.at[k], landing(7 - k), send_sem, recv_sem).wait_send()
            push(7 - k, send.at[k], landing(k), send_sem, recv_sem).wait_recv()

    each(finish)


def back(done, spots, own):
    sd = jax.ShapeDtypeStruct
    return pl.pallas_call(
        back_kernel,
        name="back",
        in_specs=[VM] * 3,
        out_specs=[VM, VM],
        out_shape=[sd((C, PTS), BF), sd((C, 8 * CAP), BF)],
        scratch_shapes=[
            pltpu.VMEM((PTS, BLOCK), BF),
            pltpu.VMEM((PTS, BLOCK), BF),
            pltpu.VMEM((8, C, CAP), BF),
            pltpu.SemaphoreType.DMA((8,)),
            pltpu.SemaphoreType.DMA((8,)),
        ],
        compiler_params=params(collective_id=2, has_side_effects=True),
    )(done, spots, own)


WIDE = 1024


def collect_kernel(kept_ref, returned_ref, away_ref, out_ref, onehot_a, onehot_b):
    i = pl.program_id(0)
    halves = ((0, onehot_a), (BLOCK, onehot_b))
    for at, onehot in halves:
        first = i * (WIDE // 128) + at // 128
        select_columns(index_row(away_ref, first, BLOCK // 128), onehot)
    for at, onehot in halves:
        taken = jnp.dot(returned_ref[...], onehot[...], preferred_element_type=F32)
        kept = kept_ref[:, at : at + BLOCK].astype(F32)
        out_ref[:, at : at + BLOCK] = (kept + taken).astype(BF)


def collect(kept, returned, away):
    return pl.pallas_call(
        collect_kernel,
        name="collect",
        grid=(PTS // WIDE,),
        in_specs=[
            pl.BlockSpec((C, WIDE), lambda i: (0, i)),
            pl.BlockSpec((C, 8 * CAP), lambda i: (0, 0)),
            pl.BlockSpec((32, 128), lambda i: (0, 0)),
        ],
        out_specs=pl.BlockSpec((C, WIDE), lambda i: (0, i)),
        out_shape=jax.ShapeDtypeStruct((C, PTS), BF),
        scratch_shapes=[pltpu.VMEM((8 * CAP, BLOCK), BF), pltpu.VMEM((8 * CAP, BLOCK), BF)],
        compiler_params=params(dimension_semantics=("arbitrary",)),
    )(kept, returned, away)


def on_device(
    feats, conv_weight, tap_index, halo_rows, hilbert_pos,
    ln1_gain, qkv_weight, out_weight, ln2_gain, mlp_in, mlp_out,
):
    feats_t = feats.T
    tap_t = tap_index.T
    halo, fetch, own, away, spot, groups, cwt, qkvt, owt, g1, g2, w1t = halo_exchange(
        halo_rows[0], feats_t, hilbert_pos.reshape(32, 128), tap_t,
        conv_weight.reshape(TAPS * C, C), qkv_weight, out_weight,
        ln1_gain.reshape(1, C), ln2_gain.reshape(1, C), mlp_in,
    )
    updated = conv(groups, spot, tap_t, cwt, feats_t, halo)
    ordered, spots = deal(updated, fetch)
    done = windows(ordered, g1, qkvt, owt, g2, w1t, mlp_out.T)
    kept, returned = back(done, spots, own)
    return collect(kept, returned, away).T


def solution(mesh):
    rows = P(("gx", "gy"), None)
    placed = (rows, P(), rows, P(("gx", "gy"), None, None), P(("gx", "gy"))) + (P(),) * 6
    return jax.shard_map(
        on_device, mesh=mesh, in_specs=placed, out_specs=rows, check_vma=False
    )
```

```python
import functools
import math

import jax
import jax.numpy as jnp
from jax import lax
from jax.experimental import pallas as pl
from jax.experimental.pallas import tpu as pltpu
from jax.sharding import PartitionSpec as P

BF = jnp.bfloat16
F32 = jnp.float32
I32 = jnp.int32
MESH = pl.DeviceIdType.MESH

C = 192
HEADS = 8
HD = 24
HP = 32
WIN = 1024
TAPS = 27
PTS = 4096
HB = 512
CAP = PTS // 16
GROUP = 128
ROWS = C + 16
VMEM_LIMIT = 60 * 1024 * 1024
SCALE = 1.0 / math.sqrt(HD) * math.log2(math.e)
SAFE = 80.0


def params(**kw):
    return pltpu.CompilerParams(vmem_limit_bytes=VMEM_LIMIT, **kw)


VM = pl.BlockSpec(memory_space=pltpu.VMEM)
SM = pl.BlockSpec(memory_space=pltpu.SMEM)
ANY = pl.BlockSpec(memory_space=pl.ANY)


def neighbour(k):
    j = k + k // 4
    x = lax.axis_index("gx") + j // 3 - 1
    y = lax.axis_index("gy") + j % 3 - 1
    inside = (x >= 0) & (x < lax.axis_size("gx")) & (y >= 0) & (y < lax.axis_size("gy"))
    return inside, x, y


def in_turn(i):
    return i + jnp.minimum(i, 1) - 3 * (i // 3)


def greet():
    barrier = pltpu.get_barrier_semaphore()
    count = jnp.int32(0)
    for k in range(8):
        inside, x, y = neighbour(k)
        count = count + inside.astype(I32)

        @pl.when(inside)
        def _():
            pl.semaphore_signal(barrier, inc=1, device_id=(x, y), device_id_type=MESH)

    return barrier, count


def push(k, src, dst, send_sem, recv_sem):
    _, x, y = neighbour(k)
    return pltpu.make_async_remote_copy(
        src_ref=src, dst_ref=dst, send_sem=send_sem.at[k], recv_sem=recv_sem.at[7 - k],
        device_id=(x, y), device_id_type=MESH,
    )


def each(body):
    def step(k, carry):
        body(k)
        return carry

    lax.fori_loop(0, 8, step, 0)


def index_row(ref, first, count):
    return jnp.concatenate([ref[pl.ds(first + u, 1), :] for u in range(count)], 1)


def select_columns(index, onehot):
    depth, width = onehot.shape
    for s in range(0, depth, 256):
        place = lax.broadcasted_iota(I32, (256, width), 0) + s
        onehot[s : s + 256, :] = jnp.where(place == index, 1.0, 0.0).astype(BF)


def spread_index(row):
    return jnp.broadcast_to(row, (128, row.shape[1])).T


def place_rows(index, base, onehot):
    depth, width = onehot.shape
    for s in range(0, depth, 256):
        here = index[s : s + 256, :] - base
        hits = [
            jnp.where(lax.broadcasted_iota(I32, (256, 128), 1) + d == here, 1.0, 0.0)
            for d in range(0, width, 128)
        ]
        onehot[s : s + 256, :] = jnp.concatenate(hits, 1).astype(BF)


def prepare_indices(hp_ref, tap_ref, fetch_ref, own_ref, away_ref, spot_ref, group_ref):
    ix = lax.axis_index("gx")
    iy = lax.axis_index("gy")
    ny = lax.axis_size("gy")
    hp = hp_ref[...]
    target = hp // PTS
    local = hp - target * PTS
    step_x = target // ny - ix
    step_y = target % ny - iy
    code = 3 * (step_x + 1) + (step_y + 1)
    r128 = lax.broadcasted_iota(I32, (128, 128), 0)
    c128 = lax.broadcasted_iota(I32, (128, 128), 1)
    tri = (r128 < c128).astype(F32).astype(BF)
    r32 = lax.broadcasted_iota(I32, (32, 32), 0)
    c32 = lax.broadcasted_iota(I32, (32, 32), 1)
    low = (c32 < r32).astype(F32).astype(BF)
    before = jnp.zeros((32, 128), F32)
    for c in range(9):
        if c == 4:
            continue
        m = (code == c).astype(F32)
        mb = m.astype(BF)
        within = jnp.dot(mb, tri, preferred_element_type=F32)
        above = jnp.sum(jnp.dot(low, mb, preferred_element_type=F32), 1, keepdims=True)
        before = before + m * (within + above)
    away = (code - (code > 4).astype(I32)) * CAP + before.astype(I32)
    own = code == 4
    fetch_ref[...] = jnp.where(own, local, PTS + away)
    own_ref[...] = jnp.where(own, local, -1)
    away_ref[...] = jnp.where(own, -1, away)
    spot_ref[...] = local
    lane = lax.broadcasted_iota(I32, (TAPS, 128), 1)
    groups = jnp.zeros((TAPS, 128), I32)
    for i in range(PTS // 128):
        top = jnp.max(tap_ref[:, i * 128 : (i + 1) * 128], 1, keepdims=True)
        groups = jnp.where(lane == i, jnp.maximum(top, 0) // 128, groups)
    group_ref[...] = groups


def prepare_weights(
    cw_ref, qkvw_ref, ow_ref, g1_ref, g2_ref, w1_ref, cwt_ref, qkvt_ref, owt_ref, g1c_ref, g2c_ref, w1t_ref, pad
):
    for i in range(0, TAPS * C, 384):
        size = min(384, TAPS * C - i)
        cwt_ref[:, i : i + size] = cw_ref[i : i + size, :].astype(F32).T.astype(BF)
    wide = qkvw_ref[...].astype(F32).T
    pad[...] = jnp.zeros_like(pad)
    for j in range(3 * HEADS):
        pad[j * HP : j * HP + HD, :] = wide[j * HD : (j + 1) * HD, :]
    qkvt_ref[...] = pad[...].astype(BF)
    ow = ow_ref[...].astype(F32)
    for j in range(HEADS):
        pad[j * HP : j * HP + HD, :] = ow[j * HD : (j + 1) * HD, :]
    owt_ref[...] = pad[0 : HEADS * HP, :].T.astype(BF)
    g1c_ref[...] = jnp.broadcast_to(g1_ref[...], (128, C)).T
    g2c_ref[...] = jnp.broadcast_to(g2_ref[...], (128, C)).T
    w1t_ref[...] = w1_ref[...].astype(F32).T.astype(BF)


def halo_kernel(
    halo_ref, feats_ref, hp_ref, tap_ref, cw_ref, qkvw_ref, ow_ref, g1_ref, g2_ref, w1_ref,
    out_ref, fetch_ref, own_ref, away_ref, spot_ref, group_ref,
    cwt_ref, qkvt_ref, owt_ref, g1c_ref, g2c_ref, w1t_ref,
    onehot, send, zeros, pad, cw, qkvw, ow, w1, tap, cwt, send_sem, recv_sem, zero_sem, load_sem,
):
    barrier, count = greet()
    loads = [
        pltpu.make_async_copy(src, dst, load_sem.at[i])
        for i, (src, dst) in enumerate(
            ((cw_ref, cw), (qkvw_ref, qkvw), (ow_ref, ow), (w1_ref, w1), (tap_ref, tap))
        )
    ]
    for load in loads:
        load.start()
    zeros[...] = jnp.zeros_like(zeros)

    def start(k):
        inside = neighbour(k)[0]

        @pl.when(inside)
        def _():
            push(k, send.at[k], out_ref.at[7 - k], send_sem, recv_sem).start()

        @pl.when(jnp.logical_not(inside))
        def _():
            pltpu.make_async_copy(zeros, out_ref.at[k], zero_sem.at[k]).start()

    def fill(k):
        select_columns(halo_ref[pl.ds(k, 1), :], onehot)
        send[k] = jnp.dot(feats_ref[...], onehot[...], preferred_element_type=F32).astype(BF)

    def one(i, carry):
        pair = in_turn(i // 2)
        k = jnp.where(i % 2 == 0, pair, 7 - pair)
        fill(k)
        start(k)
        return carry

    fill(0)
    pl.semaphore_wait(barrier, count)
    start(0)
    lax.fori_loop(1, 8, one, 0)
    for load in loads:
        load.wait()
    prepare_weights(cw, qkvw, ow, g1_ref, g2_ref, w1, cwt, qkvt_ref, owt_ref, g1c_ref, g2c_ref, w1t_ref, pad)
    store = pltpu.make_async_copy(cwt, cwt_ref, load_sem.at[5])
    store.start()
    prepare_indices(hp_ref, tap, fetch_ref, own_ref, away_ref, spot_ref, group_ref)

    def finish(k):
        inside = neighbour(k)[0]

        @pl.when(inside)
        def _():
            push(k, send.at[k], out_ref.at[7 - k], send_sem, recv_sem).wait_send()
            push(7 - k, send.at[k], out_ref.at[k], send_sem, recv_sem).wait_recv()

        @pl.when(jnp.logical_not(inside))
        def _():
            pltpu.make_async_copy(zeros, out_ref.at[k], zero_sem.at[k]).wait()

    each(finish)
    store.wait()


def halo_exchange(halo, feats_t, hp, tap_t, cw, qkvw, ow, g1, g2, w1):
    sd = jax.ShapeDtypeStruct
    return pl.pallas_call(
        halo_kernel,
        name="halo_exchange",
        in_specs=[VM, VM, VM, ANY, ANY, ANY, ANY, VM, VM, ANY],
        out_specs=[ANY] + [VM] * 5 + [ANY] + [VM] * 5,
        out_shape=[
            sd((8, C, HB), BF),
            sd((32, 128), I32), sd((32, 128), I32), sd((32, 128), I32), sd((32, 128), I32),
            sd((TAPS, 128), I32),
            sd((C, TAPS * C), BF), sd((3 * HEADS * HP, C), BF), sd((C, HEADS * HP), BF),
            sd((C, 128), F32), sd((C, 128), F32), sd((4 * C, C), BF),
        ],
        scratch_shapes=[
            pltpu.VMEM((PTS, HB), BF),
            pltpu.VMEM((8, C, HB), BF),
            pltpu.VMEM((C, HB), BF),
            pltpu.VMEM((3 * HEADS * HP, C), F32),
            pltpu.VMEM((TAPS * C, C), BF),
            pltpu.VMEM((C, 3 * C), BF),
            pltpu.VMEM((C, C), BF),
            pltpu.VMEM((C, 4 * C), BF),
            pltpu.VMEM((TAPS, PTS), I32),
            pltpu.VMEM((C, TAPS * C), BF),
            pltpu.SemaphoreType.DMA((8,)),
            pltpu.SemaphoreType.DMA((8,)),
            pltpu.SemaphoreType.DMA((8,)),
            pltpu.SemaphoreType.DMA((6,)),
        ],
        compiler_params=params(collective_id=0, has_side_effects=True),
    )(halo, feats_t, hp, tap_t, cw, qkvw, ow, g1, g2, w1)


STEP = 2
PART = 128 * STEP
PARTS = PTS // PART


def conv_kernel(
    group_ref, spot_ref, tap_ref, cwt_ref, feats_ref, halo_ref, out_ref, lookup, even, odd, cwt, load_sem,
):
    weights = pltpu.make_async_copy(cwt_ref, cwt, load_sem.at[9])
    copies = [
        pltpu.make_async_copy(feats_ref, lookup.at[:, 0:PTS], load_sem.at[8]),
    ]
    for k in range(8):
        at = PTS + k * HB
        copies.append(
            pltpu.make_async_copy(halo_ref.at[k], lookup.at[:, at : at + HB], load_sem.at[k])
        )
    for copy in copies:
        copy.start()
    weights.start()
    for r in range(PTS // 128):
        spot = spot_ref[r : r + 1, :] + 1
        number = lax.broadcasted_iota(I32, (ROWS - C, 128), 0)
        digits = jnp.where(number == 0, spot // 64, jnp.where(number == 1, spot % 64, 0))
        out_ref[C:ROWS, r * 128 : (r + 1) * 128] = digits.astype(F32).astype(BF)
    for copy in copies:
        copy.wait()
    weights.wait()

    def gather(i, gathered):
        for n in range(STEP):
            for t in range(TAPS):
                start = pl.multiple_of(group_ref[t, i * STEP + n] * 128, 128)
                source = lookup[:, pl.ds(start, 128)].astype(F32)
                lanes = pl.ds(pl.multiple_of(i * PART + n * 128, 128), 128)
                index = jnp.broadcast_to(tap_ref[t : t + 1, lanes], (C, 128))
                taken = jnp.take_along_axis(source, index & 127, axis=1)
                taken = jnp.where(index >= 0, taken, 0.0)
                gathered[t * C : (t + 1) * C, n * 128 : (n + 1) * 128] = taken.astype(BF)

    def multiply(i, gathered):
        at = pl.ds(pl.multiple_of(i * PART, PART), PART)
        conv = jnp.dot(cwt[...], gathered[...], preferred_element_type=F32)
        out_ref[0:C, at] = (lookup[:, at].astype(F32) + conv).astype(BF)

    def two(j, carry):
        multiply(jnp.maximum(2 * j - 1, 0), odd)
        gather(2 * j, even)
        multiply(2 * j, even)
        gather(2 * j + 1, odd)
        return carry

    odd[...] = jnp.zeros_like(odd)
    lax.fori_loop(0, PARTS // 2, two, 0)
    multiply(PARTS - 1, odd)


def conv(groups, spot, tap_t, cwt, feats_t, halo):
    return pl.pallas_call(
        conv_kernel,
        name="conv",
        in_specs=[SM, VM, VM, ANY, ANY, ANY],
        out_specs=VM,
        out_shape=jax.ShapeDtypeStruct((ROWS, PTS), BF),
        scratch_shapes=[
            pltpu.VMEM((C, PTS + 8 * HB), BF),
            pltpu.VMEM((TAPS * C, PART), BF),
            pltpu.VMEM((TAPS * C, PART), BF),
            pltpu.VMEM((C, TAPS * C), BF),
            pltpu.SemaphoreType.DMA((10,)),
        ],
        compiler_params=params(),
    )(groups, spot, tap_t, cwt, feats_t, halo)


BLOCK = 512


def deal_kernel(
    updated_ref, fetch_ref, out_ref, spots_ref, index, onehot_a, onehot_b, send, recv, send_sem, recv_sem
):
    barrier, count = greet()

    def landing(k):
        return recv.at[:, pl.ds(pl.multiple_of(k * CAP, CAP), CAP)]

    def blank(k):
        @pl.when(jnp.logical_not(neighbour(k)[0]))
        def _():
            recv[:, pl.ds(pl.multiple_of(k * CAP, CAP), CAP)] = jnp.zeros((ROWS, CAP), BF)

    each(blank)

    def start(k):
        @pl.when(neighbour(k)[0])
        def _():
            push(k, send.at[k], landing(7 - k), send_sem, recv_sem).start()

    for r in range(PTS // 128):
        index[r * 128 : (r + 1) * 128, :] = spread_index(fetch_ref[r : r + 1, :])
    first = onehot_a.at[:, 0:CAP]
    second = onehot_b.at[:, 0:CAP]

    def fill(k):
        place_rows(index, PTS + k * CAP, first)
        place_rows(index, PTS + (7 - k) * CAP, second)

        send[k] = jnp.dot(updated_ref[...], first[...], preferred_element_type=F32).astype(BF)
        send[7 - k] = jnp.dot(updated_ref[...], second[...], preferred_element_type=F32).astype(BF)

    def pair(i, carry):
        k = in_turn(i)
        fill(k)
        start(k)
        start(7 - k)
        return carry

    fill(0)
    pl.semaphore_wait(barrier, count)
    start(0)
    start(7)
    lax.fori_loop(1, 4, pair, 0)

    def stay(m, carry):
        for n, onehot in ((2 * m, onehot_a), (2 * m + 1, onehot_b)):
            place_rows(index, n * BLOCK, onehot)
        for n, onehot in ((2 * m, onehot_a), (2 * m + 1, onehot_b)):
            taken = jnp.dot(updated_ref[0:C, :], onehot[...], preferred_element_type=F32)
            out_ref[:, pl.ds(pl.multiple_of(n * BLOCK, BLOCK), BLOCK)] = taken.astype(BF)
        return carry

    lax.fori_loop(0, PTS // BLOCK // 2, stay, 0)

    def finish(k):
        @pl.when(neighbour(k)[0])
        def _():
            push(k, send.at[k], landing(7 - k), send_sem, recv_sem).wait_send()
            push(7 - k, send.at[k], landing(k), send_sem, recv_sem).wait_recv()

    each(finish)

    depth = 8 * CAP
    for k in range(8):
        digits = recv[C:ROWS, k * CAP : (k + 1) * CAP].astype(F32)
        spot = (digits[0:1, :] * 64.0 + digits[1:2, :] - 1.0).astype(I32)
        spots_ref[k : k + 1, :] = spot
        for c in range(0, CAP, 128):
            at = k * CAP + c
            index[at : at + 128, :] = spread_index(spot[:, c : c + 128])

    def arrive(m, carry):
        blocks = ((2 * m, onehot_a), (2 * m + 1, onehot_b))
        for n, onehot in blocks:
            place_rows(index, n * BLOCK, onehot.at[0:depth, :])
        for n, onehot in blocks:
            at = pl.ds(pl.multiple_of(n * BLOCK, BLOCK), BLOCK)
            taken = jnp.dot(recv[0:C, :], onehot[0:depth, :], preferred_element_type=F32)
            out_ref[:, at] = (out_ref[:, at].astype(F32) + taken).astype(BF)
        return carry

    lax.fori_loop(0, PTS // BLOCK // 2, arrive, 0)


def deal(updated, fetch):
    sd = jax.ShapeDtypeStruct
    return pl.pallas_call(
        deal_kernel,
        name="deal",
        in_specs=[VM, VM],
        out_specs=[VM, VM],
        out_shape=[sd((C, PTS), BF), sd((8, CAP), I32)],
        scratch_shapes=[
            pltpu.VMEM((PTS, 128), I32),
            pltpu.VMEM((PTS, BLOCK), BF),
            pltpu.VMEM((PTS, BLOCK), BF),
            pltpu.VMEM((8, ROWS, CAP), BF),
            pltpu.VMEM((ROWS, 8 * CAP), BF),
            pltpu.SemaphoreType.DMA((8,)),
            pltpu.SemaphoreType.DMA((8,)),
        ],
        compiler_params=params(collective_id=1, has_side_effects=True),
    )(updated, fetch)


def norm_columns(values, gain):
    average = jnp.sum(values, 0, keepdims=True) * (1.0 / C)
    centred = values - average
    variance = jnp.sum(centred * centred, 0, keepdims=True) * (1.0 / C)
    return (centred * lax.rsqrt(variance + 1e-05) * gain).astype(BF)


def window_kernel(
    in_ref, g1_ref, qkvt_ref, owt_ref, g2_ref, w1t_ref, w2t_ref, out_ref, packed, attended
):
    x = in_ref[...].astype(F32)
    normed = norm_columns(x, g1_ref[:, 0:1])
    wide = HEADS * HP
    queries = jnp.dot(qkvt_ref[0:wide, :], normed, preferred_element_type=F32) * SCALE
    packed[0:wide, :] = queries.astype(BF)
    packed[wide : 3 * wide, :] = jnp.dot(
        qkvt_ref[wide : 3 * wide, :], normed, preferred_element_type=F32
    ).astype(BF)
    largest_q = jnp.zeros((1, WIN), F32)
    largest_k = jnp.zeros((1, WIN), F32)
    for h in range(HEADS):
        q = packed[h * HP : (h + 1) * HP, :].astype(F32)
        key = packed[wide + h * HP : wide + (h + 1) * HP, :].astype(F32)
        largest_q = jnp.maximum(largest_q, jnp.sum(q * q, 0, keepdims=True))
        largest_k = jnp.maximum(largest_k, jnp.sum(key * key, 0, keepdims=True))
    safe = jnp.max(largest_q) * jnp.max(largest_k) <= SAFE * SAFE

    def heads(shifted):
        def head(h, inner):
            off = pl.multiple_of(h * HP, HP)
            q = packed[pl.ds(off, HP), :]
            key = packed[pl.ds(wide + off, HP), :]
            value = packed[pl.ds(2 * wide + off, HP), :]
            number = lax.broadcasted_iota(I32, (HP, WIN), 0)
            value = jnp.where(number == HD, jnp.ones_like(value), value)
            scores = lax.dot_general(
                key, q, (((0,), (0,)), ((), ())), preferred_element_type=F32
            )
            if shifted:
                scores = scores - jnp.max(scores, 0, keepdims=True)
            probs = jnp.exp2(scores).astype(BF)
            mixed = jnp.dot(value, probs, preferred_element_type=F32)
            attended[pl.ds(off, HP), :] = (mixed / mixed[HD : HD + 1, :]).astype(BF)
            return inner

        lax.fori_loop(0, HEADS, head, 0, unroll=1 if shifted else 8)

    @pl.when(safe)
    def _():
        heads(False)

    @pl.when(jnp.logical_not(safe))
    def _():
        heads(True)

    residual = x + jnp.dot(owt_ref[...], attended[...], preferred_element_type=F32)
    residual = residual.astype(BF).astype(F32)
    normed_two = norm_columns(residual, g2_ref[:, 0:1])
    hidden = jnp.dot(w1t_ref[...], normed_two, preferred_element_type=F32)
    hidden = 0.5 * hidden * (1.0 + lax.erf(hidden * (2.0**-0.5)))
    processed = residual + jnp.dot(w2t_ref[...], hidden.astype(BF), preferred_element_type=F32)
    out_ref[...] = processed.astype(BF)


def windows(ordered, g1, qkvt, owt, g2, w1t, w2t):
    return pl.pallas_call(
        window_kernel,
        name="windows",
        grid=(PTS // WIN,),
        in_specs=[pl.BlockSpec((C, WIN), lambda i: (0, i)), VM, VM, VM, VM, VM, VM],
        out_specs=pl.BlockSpec((C, WIN), lambda i: (0, i)),
        out_shape=jax.ShapeDtypeStruct((C, PTS), BF),
        scratch_shapes=[
            pltpu.VMEM((3 * HEADS * HP, WIN), BF),
            pltpu.VMEM((HEADS * HP, WIN), BF),
        ],
        compiler_params=params(dimension_semantics=("arbitrary",)),
    )(ordered, g1, qkvt, owt, g2, w1t, w2t)


def back_kernel(done_ref, spots_ref, own_ref, out_ref, recv, onehot_a, onehot_b, send, send_sem, recv_sem):
    barrier, count = greet()

    def landing(k):
        return recv.at[:, pl.ds(pl.multiple_of(k * CAP, CAP), CAP)]

    def blank(k):
        @pl.when(jnp.logical_not(neighbour(k)[0]))
        def _():
            recv[:, pl.ds(pl.multiple_of(k * CAP, CAP), CAP)] = jnp.zeros((C, CAP), BF)

    each(blank)

    def start(k):
        @pl.when(neighbour(k)[0])
        def _():
            push(k, send.at[k], landing(7 - k), send_sem, recv_sem).start()

    first = onehot_a.at[:, 0:CAP]
    second = onehot_b.at[:, 0:CAP]

    def fill(k):
        select_columns(spots_ref[pl.ds(k, 1), :], first)
        select_columns(spots_ref[pl.ds(7 - k, 1), :], second)

        send[k] = jnp.dot(done_ref[...], first[...], preferred_element_type=F32).astype(BF)
        send[7 - k] = jnp.dot(done_ref[...], second[...], preferred_element_type=F32).astype(BF)

    def pair(i, carry):
        k = in_turn(i)
        fill(k)
        start(k)
        start(7 - k)
        return carry

    fill(0)
    pl.semaphore_wait(barrier, count)
    start(0)
    start(7)
    lax.fori_loop(1, 4, pair, 0)

    def stay(m, carry):
        for n, onehot in ((2 * m, onehot_a), (2 * m + 1, onehot_b)):
            select_columns(index_row(own_ref, n * (BLOCK // 128), BLOCK // 128), onehot)
        for n, onehot in ((2 * m, onehot_a), (2 * m + 1, onehot_b)):
            taken = jnp.dot(done_ref[...], onehot[...], preferred_element_type=F32)
            out_ref[:, pl.ds(pl.multiple_of(n * BLOCK, BLOCK), BLOCK)] = taken.astype(BF)
        return carry

    lax.fori_loop(0, PTS // BLOCK // 2, stay, 0)

    def finish(k):
        @pl.when(neighbour(k)[0])
        def _():
            push(k, send.at[k], landing(7 - k), send_sem, recv_sem).wait_send()
            push(7 - k, send.at[k], landing(k), send_sem, recv_sem).wait_recv()

    each(finish)


def back(done, spots, own):
    sd = jax.ShapeDtypeStruct
    return pl.pallas_call(
        back_kernel,
        name="back",
        in_specs=[VM] * 3,
        out_specs=[VM, VM],
        out_shape=[sd((C, PTS), BF), sd((C, 8 * CAP), BF)],
        scratch_shapes=[
            pltpu.VMEM((PTS, BLOCK), BF),
            pltpu.VMEM((PTS, BLOCK), BF),
            pltpu.VMEM((8, C, CAP), BF),
            pltpu.SemaphoreType.DMA((8,)),
            pltpu.SemaphoreType.DMA((8,)),
        ],
        compiler_params=params(collective_id=2, has_side_effects=True),
    )(done, spots, own)


WIDE = 1024


def collect_kernel(kept_ref, returned_ref, away_ref, out_ref, onehot_a, onehot_b):
    i = pl.program_id(0)
    halves = ((0, onehot_a), (BLOCK, onehot_b))
    for at, onehot in halves:
        first = i * (WIDE // 128) + at // 128
        select_columns(index_row(away_ref, first, BLOCK // 128), onehot)
    for at, onehot in halves:
        taken = jnp.dot(returned_ref[...], onehot[...], preferred_element_type=F32)
        kept = kept_ref[:, at : at + BLOCK].astype(F32)
        out_ref[:, at : at + BLOCK] = (kept + taken).astype(BF)


def collect(kept, returned, away):
    return pl.pallas_call(
        collect_kernel,
        name="collect",
        grid=(PTS // WIDE,),
        in_specs=[
            pl.BlockSpec((C, WIDE), lambda i: (0, i)),
            pl.BlockSpec((C, 8 * CAP), lambda i: (0, 0)),
            pl.BlockSpec((32, 128), lambda i: (0, 0)),
        ],
        out_specs=pl.BlockSpec((C, WIDE), lambda i: (0, i)),
        out_shape=jax.ShapeDtypeStruct((C, PTS), BF),
        scratch_shapes=[pltpu.VMEM((8 * CAP, BLOCK), BF), pltpu.VMEM((8 * CAP, BLOCK), BF)],
        compiler_params=params(dimension_semantics=("arbitrary",)),
    )(kept, returned, away)


def on_device(
    feats, conv_weight, tap_index, halo_rows, hilbert_pos,
    ln1_gain, qkv_weight, out_weight, ln2_gain, mlp_in, mlp_out,
):
    feats_t = feats.T
    tap_t = tap_index.T
    halo, fetch, own, away, spot, groups, cwt, qkvt, owt, g1, g2, w1t = halo_exchange(
        halo_rows[0], feats_t, hilbert_pos.reshape(32, 128), tap_t,
        conv_weight.reshape(TAPS * C, C), qkv_weight, out_weight,
        ln1_gain.reshape(1, C), ln2_gain.reshape(1, C), mlp_in,
    )
    updated = conv(groups, spot, tap_t, cwt, feats_t, halo)
    ordered, spots = deal(updated, fetch)
    done = windows(ordered, g1, qkvt, owt, g2, w1t, mlp_out.T)
    kept, returned = back(done, spots, own)
    return collect(kept, returned, away).T


def solution(mesh):
    rows = P(("gx", "gy"), None)
    placed = (rows, P(), rows, P(("gx", "gy"), None, None), P(("gx", "gy"))) + (P(),) * 6
    return jax.shard_map(
        on_device, mesh=mesh, in_specs=placed, out_specs=rows, check_vma=False
    )
```

```python
import functools
import math

import jax
import jax.numpy as jnp
from jax import lax
from jax.experimental import pallas as pl
from jax.experimental.pallas import tpu as pltpu
from jax.sharding import PartitionSpec as P

BF = jnp.bfloat16
F32 = jnp.float32
I32 = jnp.int32
MESH = pl.DeviceIdType.MESH

C = 192
HEADS = 8
HD = 24
HP = 32
WIN = 1024
TAPS = 27
PTS = 4096
HB = 512
CAP = PTS // 16
GROUP = 128
ROWS = C + 16
VMEM_LIMIT = 60 * 1024 * 1024
SCALE = 1.0 / math.sqrt(HD) * math.log2(math.e)
SAFE = 80.0


def params(**kw):
    return pltpu.CompilerParams(vmem_limit_bytes=VMEM_LIMIT, **kw)


VM = pl.BlockSpec(memory_space=pltpu.VMEM)
SM = pl.BlockSpec(memory_space=pltpu.SMEM)
ANY = pl.BlockSpec(memory_space=pl.ANY)


def neighbour(k):
    j = k + k // 4
    x = lax.axis_index("gx") + j // 3 - 1
    y = lax.axis_index("gy") + j % 3 - 1
    inside = (x >= 0) & (x < lax.axis_size("gx")) & (y >= 0) & (y < lax.axis_size("gy"))
    return inside, x, y


def in_turn(i):
    return i + jnp.minimum(i, 1) - 3 * (i // 3)


def greet():
    barrier = pltpu.get_barrier_semaphore()
    count = jnp.int32(0)
    for k in range(8):
        inside, x, y = neighbour(k)
        count = count + inside.astype(I32)

        @pl.when(inside)
        def _():
            pl.semaphore_signal(barrier, inc=1, device_id=(x, y), device_id_type=MESH)

    return barrier, count


def push(k, src, dst, send_sem, recv_sem):
    _, x, y = neighbour(k)
    return pltpu.make_async_remote_copy(
        src_ref=src, dst_ref=dst, send_sem=send_sem.at[k], recv_sem=recv_sem.at[7 - k],
        device_id=(x, y), device_id_type=MESH,
    )


def each(body):
    def step(k, carry):
        body(k)
        return carry

    lax.fori_loop(0, 8, step, 0)


def index_row(ref, first, count):
    return jnp.concatenate([ref[pl.ds(first + u, 1), :] for u in range(count)], 1)


def select_columns(index, onehot):
    depth, width = onehot.shape
    for s in range(0, depth, 256):
        place = lax.broadcasted_iota(I32, (256, width), 0) + s
        onehot[s : s + 256, :] = jnp.where(place == index, 1.0, 0.0).astype(BF)


def spread_index(row):
    return jnp.broadcast_to(row, (128, row.shape[1])).T


def place_rows(index, base, onehot):
    depth, width = onehot.shape
    for s in range(0, depth, 256):
        here = index[s : s + 256, :] - base
        hits = [
            jnp.where(lax.broadcasted_iota(I32, (256, 128), 1) + d == here, 1.0, 0.0)
            for d in range(0, width, 128)
        ]
        onehot[s : s + 256, :] = jnp.concatenate(hits, 1).astype(BF)


def prepare_indices(hp_ref, tap_ref, fetch_ref, own_ref, away_ref, spot_ref, group_ref):
    ix = lax.axis_index("gx")
    iy = lax.axis_index("gy")
    ny = lax.axis_size("gy")
    hp = hp_ref[...]
    target = hp // PTS
    local = hp - target * PTS
    step_x = target // ny - ix
    step_y = target % ny - iy
    code = 3 * (step_x + 1) + (step_y + 1)
    r128 = lax.broadcasted_iota(I32, (128, 128), 0)
    c128 = lax.broadcasted_iota(I32, (128, 128), 1)
    tri = (r128 < c128).astype(F32).astype(BF)
    r32 = lax.broadcasted_iota(I32, (32, 32), 0)
    c32 = lax.broadcasted_iota(I32, (32, 32), 1)
    low = (c32 < r32).astype(F32).astype(BF)
    before = jnp.zeros((32, 128), F32)
    for c in range(9):
        if c == 4:
            continue
        m = (code == c).astype(F32)
        mb = m.astype(BF)
        within = jnp.dot(mb, tri, preferred_element_type=F32)
        above = jnp.sum(jnp.dot(low, mb, preferred_element_type=F32), 1, keepdims=True)
        before = before + m * (within + above)
    away = (code - (code > 4).astype(I32)) * CAP + before.astype(I32)
    own = code == 4
    fetch_ref[...] = jnp.where(own, local, PTS + away)
    own_ref[...] = jnp.where(own, local, -1)
    away_ref[...] = jnp.where(own, -1, away)
    spot_ref[...] = local
    lane = lax.broadcasted_iota(I32, (TAPS, 128), 1)
    groups = jnp.zeros((TAPS, 128), I32)
    for i in range(PTS // 128):
        top = jnp.max(tap_ref[:, i * 128 : (i + 1) * 128], 1, keepdims=True)
        groups = jnp.where(lane == i, jnp.maximum(top, 0) // 128, groups)
    group_ref[...] = groups


def prepare_weights(
    cw_ref, qkvw_ref, ow_ref, g1_ref, g2_ref, w1_ref, cwt_ref, qkvt_ref, owt_ref, g1c_ref, g2c_ref, w1t_ref, pad
):
    for i in range(0, TAPS * C, 384):
        size = min(384, TAPS * C - i)
        cwt_ref[:, i : i + size] = cw_ref[i : i + size, :].astype(F32).T.astype(BF)
    wide = qkvw_ref[...].astype(F32).T
    pad[...] = jnp.zeros_like(pad)
    for j in range(3 * HEADS):
        pad[j * HP : j * HP + HD, :] = wide[j * HD : (j + 1) * HD, :]
    qkvt_ref[...] = pad[...].astype(BF)
    ow = ow_ref[...].astype(F32)
    for j in range(HEADS):
        pad[j * HP : j * HP + HD, :] = ow[j * HD : (j + 1) * HD, :]
    owt_ref[...] = pad[0 : HEADS * HP, :].T.astype(BF)
    g1c_ref[...] = jnp.broadcast_to(g1_ref[...], (128, C)).T
    g2c_ref[...] = jnp.broadcast_to(g2_ref[...], (128, C)).T
    w1t_ref[...] = w1_ref[...].astype(F32).T.astype(BF)


def halo_kernel(
    halo_ref, feats_ref, hp_ref, tap_ref, cw_ref, qkvw_ref, ow_ref, g1_ref, g2_ref, w1_ref,
    out_ref, fetch_ref, own_ref, away_ref, spot_ref, group_ref,
    cwt_ref, qkvt_ref, owt_ref, g1c_ref, g2c_ref, w1t_ref,
    onehot, send, zeros, pad, cw, qkvw, ow, w1, tap, cwt, send_sem, recv_sem, zero_sem, load_sem,
):
    barrier, count = greet()
    loads = [
        pltpu.make_async_copy(src, dst, load_sem.at[i])
        for i, (src, dst) in enumerate(
            ((cw_ref, cw), (qkvw_ref, qkvw), (ow_ref, ow), (w1_ref, w1), (tap_ref, tap))
        )
    ]
    for load in loads:
        load.start()
    zeros[...] = jnp.zeros_like(zeros)

    def start(k):
        inside = neighbour(k)[0]

        @pl.when(inside)
        def _():
            push(k, send.at[k], out_ref.at[7 - k], send_sem, recv_sem).start()

        @pl.when(jnp.logical_not(inside))
        def _():
            pltpu.make_async_copy(zeros, out_ref.at[k], zero_sem.at[k]).start()

    def fill(k):
        select_columns(halo_ref[pl.ds(k, 1), :], onehot)
        send[k] = jnp.dot(feats_ref[...], onehot[...], preferred_element_type=F32).astype(BF)

    def one(i, carry):
        pair = in_turn(i // 2)
        k = jnp.where(i % 2 == 0, pair, 7 - pair)
        fill(k)
        start(k)
        return carry

    fill(0)
    pl.semaphore_wait(barrier, count)
    start(0)
    lax.fori_loop(1, 8, one, 0)
    for load in loads:
        load.wait()
    prepare_weights(cw, qkvw, ow, g1_ref, g2_ref, w1, cwt, qkvt_ref, owt_ref, g1c_ref, g2c_ref, w1t_ref, pad)
    store = pltpu.make_async_copy(cwt, cwt_ref, load_sem.at[5])
    store.start()
    prepare_indices(hp_ref, tap, fetch_ref, own_ref, away_ref, spot_ref, group_ref)

    def finish(k):
        inside = neighbour(k)[0]

        @pl.when(inside)
        def _():
            push(k, send.at[k], out_ref.at[7 - k], send_sem, recv_sem).wait_send()
            push(7 - k, send.at[k], out_ref.at[k], send_sem, recv_sem).wait_recv()

        @pl.when(jnp.logical_not(inside))
        def _():
            pltpu.make_async_copy(zeros, out_ref.at[k], zero_sem.at[k]).wait()

    each(finish)
    store.wait()


def halo_exchange(halo, feats_t, hp, tap_t, cw, qkvw, ow, g1, g2, w1):
    sd = jax.ShapeDtypeStruct
    return pl.pallas_call(
        halo_kernel,
        name="halo_exchange",
        in_specs=[VM, VM, VM, ANY, ANY, ANY, ANY, VM, VM, ANY],
        out_specs=[ANY] + [VM] * 5 + [ANY] + [VM] * 5,
        out_shape=[
            sd((8, C, HB), BF),
            sd((32, 128), I32), sd((32, 128), I32), sd((32, 128), I32), sd((32, 128), I32),
            sd((TAPS, 128), I32),
            sd((C, TAPS * C), BF), sd((3 * HEADS * HP, C), BF), sd((C, HEADS * HP), BF),
            sd((C, 128), F32), sd((C, 128), F32), sd((4 * C, C), BF),
        ],
        scratch_shapes=[
            pltpu.VMEM((PTS, HB), BF),
            pltpu.VMEM((8, C, HB), BF),
            pltpu.VMEM((C, HB), BF),
            pltpu.VMEM((3 * HEADS * HP, C), F32),
            pltpu.VMEM((TAPS * C, C), BF),
            pltpu.VMEM((C, 3 * C), BF),
            pltpu.VMEM((C, C), BF),
            pltpu.VMEM((C, 4 * C), BF),
            pltpu.VMEM((TAPS, PTS), I32),
            pltpu.VMEM((C, TAPS * C), BF),
            pltpu.SemaphoreType.DMA((8,)),
            pltpu.SemaphoreType.DMA((8,)),
            pltpu.SemaphoreType.DMA((8,)),
            pltpu.SemaphoreType.DMA((6,)),
        ],
        compiler_params=params(collective_id=0, has_side_effects=True),
    )(halo, feats_t, hp, tap_t, cw, qkvw, ow, g1, g2, w1)


STEP = 2
PART = 128 * STEP
PARTS = PTS // PART


def conv_kernel(
    group_ref, spot_ref, tap_ref, cwt_ref, feats_ref, halo_ref, out_ref, lookup, even, odd, cwt, load_sem,
):
    weights = pltpu.make_async_copy(cwt_ref, cwt, load_sem.at[9])
    copies = [
        pltpu.make_async_copy(feats_ref, lookup.at[:, 0:PTS], load_sem.at[8]),
    ]
    for k in range(8):
        at = PTS + k * HB
        copies.append(
            pltpu.make_async_copy(halo_ref.at[k], lookup.at[:, at : at + HB], load_sem.at[k])
        )
    for copy in copies:
        copy.start()
    weights.start()
    for r in range(PTS // 128):
        spot = spot_ref[r : r + 1, :] + 1
        number = lax.broadcasted_iota(I32, (ROWS - C, 128), 0)
        digits = jnp.where(number == 0, spot // 64, jnp.where(number == 1, spot % 64, 0))
        out_ref[C:ROWS, r * 128 : (r + 1) * 128] = digits.astype(F32).astype(BF)
    for copy in copies:
        copy.wait()
    weights.wait()

    def gather(i, gathered):
        for n in range(STEP):
            for t in range(TAPS):
                start = pl.multiple_of(group_ref[t, i * STEP + n] * 128, 128)
                source = lookup[:, pl.ds(start, 128)].astype(F32)
                lanes = pl.ds(pl.multiple_of(i * PART + n * 128, 128), 128)
                index = jnp.broadcast_to(tap_ref[t : t + 1, lanes], (C, 128))
                taken = jnp.take_along_axis(source, index & 127, axis=1)
                taken = jnp.where(index >= 0, taken, 0.0)
                gathered[t * C : (t + 1) * C, n * 128 : (n + 1) * 128] = taken.astype(BF)

    def multiply(i, gathered):
        at = pl.ds(pl.multiple_of(i * PART, PART), PART)
        conv = jnp.dot(cwt[...], gathered[...], preferred_element_type=F32)
        out_ref[0:C, at] = (lookup[:, at].astype(F32) + conv).astype(BF)

    def two(j, carry):
        multiply(jnp.maximum(2 * j - 1, 0), odd)
        gather(2 * j, even)
        multiply(2 * j, even)
        gather(2 * j + 1, odd)
        return carry

    odd[...] = jnp.zeros_like(odd)
    lax.fori_loop(0, PARTS // 2, two, 0)
    multiply(PARTS - 1, odd)


def conv(groups, spot, tap_t, cwt, feats_t, halo):
    return pl.pallas_call(
        conv_kernel,
        name="conv",
        in_specs=[SM, VM, VM, ANY, ANY, ANY],
        out_specs=VM,
        out_shape=jax.ShapeDtypeStruct((ROWS, PTS), BF),
        scratch_shapes=[
            pltpu.VMEM((C, PTS + 8 * HB), BF),
            pltpu.VMEM((TAPS * C, PART), BF),
            pltpu.VMEM((TAPS * C, PART), BF),
            pltpu.VMEM((C, TAPS * C), BF),
            pltpu.SemaphoreType.DMA((10,)),
        ],
        compiler_params=params(),
    )(groups, spot, tap_t, cwt, feats_t, halo)


BLOCK = 512


def deal_kernel(
    updated_ref, fetch_ref, out_ref, spots_ref, index, onehot_a, onehot_b, send, recv, send_sem, recv_sem
):
    barrier, count = greet()

    def landing(k):
        return recv.at[:, pl.ds(pl.multiple_of(k * CAP, CAP), CAP)]

    def blank(k):
        @pl.when(jnp.logical_not(neighbour(k)[0]))
        def _():
            recv[:, pl.ds(pl.multiple_of(k * CAP, CAP), CAP)] = jnp.zeros((ROWS, CAP), BF)

    each(blank)

    def start(k):
        @pl.when(neighbour(k)[0])
        def _():
            push(k, send.at[k], landing(7 - k), send_sem, recv_sem).start()

    for r in range(PTS // 128):
        index[r * 128 : (r + 1) * 128, :] = spread_index(fetch_ref[r : r + 1, :])
    first = onehot_a.at[:, 0:CAP]
    second = onehot_b.at[:, 0:CAP]

    def fill(k):
        place_rows(index, PTS + k * CAP, first)
        place_rows(index, PTS + (7 - k) * CAP, second)

        send[k] = jnp.dot(updated_ref[...], first[...], preferred_element_type=F32).astype(BF)
        send[7 - k] = jnp.dot(updated_ref[...], second[...], preferred_element_type=F32).astype(BF)

    def pair(i, carry):
        k = in_turn(i)
        fill(k)
        start(k)
        start(7 - k)
        return carry

    fill(0)
    pl.semaphore_wait(barrier, count)
    start(0)
    start(7)
    lax.fori_loop(1, 4, pair, 0)

    def stay(m, carry):
        for n, onehot in ((2 * m, onehot_a), (2 * m + 1, onehot_b)):
            place_rows(index, n * BLOCK, onehot)
        for n, onehot in ((2 * m, onehot_a), (2 * m + 1, onehot_b)):
            taken = jnp.dot(updated_ref[0:C, :], onehot[...], preferred_element_type=F32)
            out_ref[:, pl.ds(pl.multiple_of(n * BLOCK, BLOCK), BLOCK)] = taken.astype(BF)
        return carry

    lax.fori_loop(0, PTS // BLOCK // 2, stay, 0)

    def finish(k):
        @pl.when(neighbour(k)[0])
        def _():
            push(k, send.at[k], landing(7 - k), send_sem, recv_sem).wait_send()
            push(7 - k, send.at[k], landing(k), send_sem, recv_sem).wait_recv()

    each(finish)

    depth = 8 * CAP
    for k in range(8):
        digits = recv[C:ROWS, k * CAP : (k + 1) * CAP].astype(F32)
        spot = (digits[0:1, :] * 64.0 + digits[1:2, :] - 1.0).astype(I32)
        spots_ref[k : k + 1, :] = spot
        for c in range(0, CAP, 128):
            at = k * CAP + c
            index[at : at + 128, :] = spread_index(spot[:, c : c + 128])

    def arrive(m, carry):
        blocks = ((2 * m, onehot_a), (2 * m + 1, onehot_b))
        for n, onehot in blocks:
            place_rows(index, n * BLOCK, onehot.at[0:depth, :])
        for n, onehot in blocks:
            at = pl.ds(pl.multiple_of(n * BLOCK, BLOCK), BLOCK)
            taken = jnp.dot(recv[0:C, :], onehot[0:depth, :], preferred_element_type=F32)
            out_ref[:, at] = (out_ref[:, at].astype(F32) + taken).astype(BF)
        return carry

    lax.fori_loop(0, PTS // BLOCK // 2, arrive, 0)


def deal(updated, fetch):
    sd = jax.ShapeDtypeStruct
    return pl.pallas_call(
        deal_kernel,
        name="deal",
        in_specs=[VM, VM],
        out_specs=[VM, VM],
        out_shape=[sd((C, PTS), BF), sd((8, CAP), I32)],
        scratch_shapes=[
            pltpu.VMEM((PTS, 128), I32),
            pltpu.VMEM((PTS, BLOCK), BF),
            pltpu.VMEM((PTS, BLOCK), BF),
            pltpu.VMEM((8, ROWS, CAP), BF),
            pltpu.VMEM((ROWS, 8 * CAP), BF),
            pltpu.SemaphoreType.DMA((8,)),
            pltpu.SemaphoreType.DMA((8,)),
        ],
        compiler_params=params(collective_id=1, has_side_effects=True),
    )(updated, fetch)


def norm_columns(values, gain):
    average = jnp.sum(values, 0, keepdims=True) * (1.0 / C)
    centred = values - average
    variance = jnp.sum(centred * centred, 0, keepdims=True) * (1.0 / C)
    return (centred * lax.rsqrt(variance + 1e-05) * gain).astype(BF)


def window_kernel(
    in_ref, g1_ref, qkvt_ref, owt_ref, g2_ref, w1t_ref, w2t_ref, out_ref, packed, attended
):
    x = in_ref[...].astype(F32)
    normed = norm_columns(x, g1_ref[:, 0:1])
    wide = HEADS * HP
    queries = jnp.dot(qkvt_ref[0:wide, :], normed, preferred_element_type=F32) * SCALE
    packed[0:wide, :] = queries.astype(BF)
    packed[wide : 3 * wide, :] = jnp.dot(
        qkvt_ref[wide : 3 * wide, :], normed, preferred_element_type=F32
    ).astype(BF)
    largest_q = jnp.zeros((1, WIN), F32)
    largest_k = jnp.zeros((1, WIN), F32)
    for h in range(HEADS):
        q = packed[h * HP : (h + 1) * HP, :].astype(F32)
        key = packed[wide + h * HP : wide + (h + 1) * HP, :].astype(F32)
        largest_q = jnp.maximum(largest_q, jnp.sum(q * q, 0, keepdims=True))
        largest_k = jnp.maximum(largest_k, jnp.sum(key * key, 0, keepdims=True))
    safe = jnp.max(largest_q) * jnp.max(largest_k) <= SAFE * SAFE

    def heads(shifted):
        def head(h, inner):
            off = pl.multiple_of(h * HP, HP)
            q = packed[pl.ds(off, HP), :]
            key = packed[pl.ds(wide + off, HP), :]
            value = packed[pl.ds(2 * wide + off, HP), :]
            number = lax.broadcasted_iota(I32, (HP, WIN), 0)
            value = jnp.where(number == HD, jnp.ones_like(value), value)
            scores = lax.dot_general(
                key, q, (((0,), (0,)), ((), ())), preferred_element_type=F32
            )
            if shifted:
                scores = scores - jnp.max(scores, 0, keepdims=True)
            probs = jnp.exp2(scores).astype(BF)
            mixed = jnp.dot(value, probs, preferred_element_type=F32)
            attended[pl.ds(off, HP), :] = (mixed / mixed[HD : HD + 1, :]).astype(BF)
            return inner

        lax.fori_loop(0, HEADS, head, 0, unroll=1 if shifted else 8)

    @pl.when(safe)
    def _():
        heads(False)

    @pl.when(jnp.logical_not(safe))
    def _():
        heads(True)

    residual = x + jnp.dot(owt_ref[...], attended[...], preferred_element_type=F32)
    residual = residual.astype(BF).astype(F32)
    normed_two = norm_columns(residual, g2_ref[:, 0:1])
    hidden = jnp.dot(w1t_ref[...], normed_two, preferred_element_type=F32)
    hidden = 0.5 * hidden * (1.0 + lax.erf(hidden * (2.0**-0.5)))
    processed = residual + jnp.dot(w2t_ref[...], hidden.astype(BF), preferred_element_type=F32)
    out_ref[...] = processed.astype(BF)


def windows(ordered, g1, qkvt, owt, g2, w1t, w2t):
    return pl.pallas_call(
        window_kernel,
        name="windows",
        grid=(PTS // WIN,),
        in_specs=[pl.BlockSpec((C, WIN), lambda i: (0, i)), VM, VM, VM, VM, VM, VM],
        out_specs=pl.BlockSpec((C, WIN), lambda i: (0, i)),
        out_shape=jax.ShapeDtypeStruct((C, PTS), BF),
        scratch_shapes=[
            pltpu.VMEM((3 * HEADS * HP, WIN), BF),
            pltpu.VMEM((HEADS * HP, WIN), BF),
        ],
        compiler_params=params(dimension_semantics=("arbitrary",)),
    )(ordered, g1, qkvt, owt, g2, w1t, w2t)


def back_kernel(done_ref, spots_ref, own_ref, out_ref, recv, onehot_a, onehot_b, send, send_sem, recv_sem):
    barrier, count = greet()

    def landing(k):
        return recv.at[:, pl.ds(pl.multiple_of(k * CAP, CAP), CAP)]

    def blank(k):
        @pl.when(jnp.logical_not(neighbour(k)[0]))
        def _():
            recv[:, pl.ds(pl.multiple_of(k * CAP, CAP), CAP)] = jnp.zeros((C, CAP), BF)

    each(blank)

    def start(k):
        @pl.when(neighbour(k)[0])
        def _():
            push(k, send.at[k], landing(7 - k), send_sem, recv_sem).start()

    first = onehot_a.at[:, 0:CAP]
    second = onehot_b.at[:, 0:CAP]

    def fill(k):
        select_columns(spots_ref[pl.ds(k, 1), :], first)
        select_columns(spots_ref[pl.ds(7 - k, 1), :], second)

        send[k] = jnp.dot(done_ref[...], first[...], preferred_element_type=F32).astype(BF)
        send[7 - k] = jnp.dot(done_ref[...], second[...], preferred_element_type=F32).astype(BF)

    def pair(i, carry):
        k = in_turn(i)
        fill(k)
        start(k)
        start(7 - k)
        return carry

    fill(0)
    pl.semaphore_wait(barrier, count)
    start(0)
    start(7)
    lax.fori_loop(1, 4, pair, 0)

    def stay(m, carry):
        for n, onehot in ((2 * m, onehot_a), (2 * m + 1, onehot_b)):
            select_columns(index_row(own_ref, n * (BLOCK // 128), BLOCK // 128), onehot)
        for n, onehot in ((2 * m, onehot_a), (2 * m + 1, onehot_b)):
            taken = jnp.dot(done_ref[...], onehot[...], preferred_element_type=F32)
            out_ref[:, pl.ds(pl.multiple_of(n * BLOCK, BLOCK), BLOCK)] = taken.astype(BF)
        return carry

    lax.fori_loop(0, PTS // BLOCK // 2, stay, 0)

    def finish(k):
        @pl.when(neighbour(k)[0])
        def _():
            push(k, send.at[k], landing(7 - k), send_sem, recv_sem).wait_send()
            push(7 - k, send.at[k], landing(k), send_sem, recv_sem).wait_recv()

    each(finish)


def back(done, spots, own):
    sd = jax.ShapeDtypeStruct
    return pl.pallas_call(
        back_kernel,
        name="back",
        in_specs=[VM] * 3,
        out_specs=[VM, VM],
        out_shape=[sd((C, PTS), BF), sd((C, 8 * CAP), BF)],
        scratch_shapes=[
            pltpu.VMEM((PTS, BLOCK), BF),
            pltpu.VMEM((PTS, BLOCK), BF),
            pltpu.VMEM((8, C, CAP), BF),
            pltpu.SemaphoreType.DMA((8,)),
            pltpu.SemaphoreType.DMA((8,)),
        ],
        compiler_params=params(collective_id=2, has_side_effects=True),
    )(done, spots, own)


WIDE = 2048


def collect_kernel(kept_ref, returned_ref, away_ref, out_ref, onehot_a, onehot_b):
    i = pl.program_id(0)
    for at in range(0, WIDE, BLOCK):
        onehot = (onehot_a, onehot_b)[at // BLOCK % 2]
        first = i * (WIDE // 128) + at // 128
        select_columns(index_row(away_ref, first, BLOCK // 128), onehot)
        taken = jnp.dot(returned_ref[...], onehot[...], preferred_element_type=F32)
        kept = kept_ref[:, at : at + BLOCK].astype(F32)
        out_ref[:, at : at + BLOCK] = (kept + taken).astype(BF)


def collect(kept, returned, away):
    return pl.pallas_call(
        collect_kernel,
        name="collect",
        grid=(PTS // WIDE,),
        in_specs=[
            pl.BlockSpec((C, WIDE), lambda i: (0, i)),
            pl.BlockSpec((C, 8 * CAP), lambda i: (0, 0)),
            pl.BlockSpec((32, 128), lambda i: (0, 0)),
        ],
        out_specs=pl.BlockSpec((C, WIDE), lambda i: (0, i)),
        out_shape=jax.ShapeDtypeStruct((C, PTS), BF),
        scratch_shapes=[pltpu.VMEM((8 * CAP, BLOCK), BF), pltpu.VMEM((8 * CAP, BLOCK), BF)],
        compiler_params=params(dimension_semantics=("arbitrary",)),
    )(kept, returned, away)


def on_device(
    feats, conv_weight, tap_index, halo_rows, hilbert_pos,
    ln1_gain, qkv_weight, out_weight, ln2_gain, mlp_in, mlp_out,
):
    feats_t = feats.T
    tap_t = tap_index.T
    halo, fetch, own, away, spot, groups, cwt, qkvt, owt, g1, g2, w1t = halo_exchange(
        halo_rows[0], feats_t, hilbert_pos.reshape(32, 128), tap_t,
        conv_weight.reshape(TAPS * C, C), qkv_weight, out_weight,
        ln1_gain.reshape(1, C), ln2_gain.reshape(1, C), mlp_in,
    )
    updated = conv(groups, spot, tap_t, cwt, feats_t, halo)
    ordered, spots = deal(updated, fetch)
    done = windows(ordered, g1, qkvt, owt, g2, w1t, mlp_out.T)
    kept, returned = back(done, spots, own)
    return collect(kept, returned, away).T


def solution(mesh):
    rows = P(("gx", "gy"), None)
    placed = (rows, P(), rows, P(("gx", "gy"), None, None), P(("gx", "gy"))) + (P(),) * 6
    return jax.shard_map(
        on_device, mesh=mesh, in_specs=placed, out_specs=rows, check_vma=False
    )
```
